256 devices in a mesh: dp: 2 (over z_lo), seq: 16 (over y, x), tensor: 8 (over z_hi, core).
Axes of the slice: x: 4, y: 4, z: 8 (z_hi: 4, z_lo: 2; z = z_hi * 2 + z_lo), core: 2. Of those that a mesh axis runs over, the one named last changes fastest.
Arguments:
- query_rows: bfloat16 [2, 3072, 3072], P('dp', 'seq', 'tensor'), may hold values from -12 to 12
- key_rows: bfloat16 [2, 3072, 3072], P('dp', 'seq', 'tensor'), may hold values from -12 to 12
- value_rows: bfloat16 [2, 3072, 3072], P('dp', 'seq', 'tensor'), may hold values from -6 to 6
- lengths: int32 [2], P('dp'), may hold values from 1536 to 3072, as said below
- out_weight: bfloat16 [3072, 3072], P('seq', 'tensor'), may hold values from -4.1875 to 4.1875
- gate_vector: float32 [2, 3072], P('dp'), may hold values from 0.5 to 1.5
- cotangent: bfloat16 [2, 3072, 3072], P('dp', 'seq', 'tensor'), may hold values from -12 to 12
Outputs:
- branch_out: bfloat16 [2, 3072, 3072], P('dp', 'seq', 'tensor')
- grad_query: bfloat16 [2, 3072, 3072], P('dp', 'seq', 'tensor')
- grad_key: bfloat16 [2, 3072, 3072], P('dp', 'seq', 'tensor')
- grad_value: bfloat16 [2, 3072, 3072], P('dp', 'seq', 'tensor')
- grad_weight: float32 [3072, 3072], P('seq', 'tensor')
- grad_gate: float32 [2, 3072], P('dp', 'tensor')
The draws below stay inside these ranges and needn't reach their ends.
Inputs may be any that keep to these rules, and one draw needn't show every extreme that they name: `lengths`: some clip has all 3072 positions live.
All inputs are finite; a program needn't handle non-finite values.
Results may differ from the reference program's by a relative error of at most 0.035.
Values may be sent and summed in bfloat16 or wider, within the bound.
A program may use at most 64 MiB of HBM per device.

```python
import math
import jax
import jax.numpy as jnp
from jax import lax

D = 3072
HEADS = 24
HD = 128
CLIPS = 2
SEQ_LEN = 3072


def drawn_pair(key):
    streams = jax.random.split(jax.random.fold_in(key, 101), 2)
    full_shape = (CLIPS, SEQ_LEN, D)
    query_mat = jnp.clip(jax.random.normal(streams[0], full_shape, jnp.float32), -6.0, 6.0)
    key_mat = jnp.clip(jax.random.normal(streams[1], full_shape, jnp.float32), -6.0, 6.0)
    return (query_mat, key_mat)


def draw_query_rows(key, part):
    return drawn_pair(key)[0].astype(jnp.bfloat16)


def draw_key_rows(key, part):
    return drawn_pair(key)[1].astype(jnp.bfloat16)


def draw_lengths(key, part):
    streams = jax.random.split(jax.random.fold_in(key, 202), 2)
    drawn_lengths = jax.random.randint(streams[0], (CLIPS,), SEQ_LEN // 2, SEQ_LEN + 1)
    full_clip = jax.random.randint(streams[1], (), 0, CLIPS)
    return jnp.where(jnp.arange(CLIPS) == full_clip, SEQ_LEN, drawn_lengths).astype(jnp.int32)


def draw_cotangent(key, part):
    streams = jax.random.split(jax.random.fold_in(key, 303), 1)
    full_shape = (CLIPS, SEQ_LEN, D)
    token_ramp = 1.0 + 2.0 * jnp.arange(SEQ_LEN, dtype=jnp.float32)[None, :, None] / (SEQ_LEN - 1)
    noise_part = jnp.clip(jax.random.normal(streams[0], full_shape, jnp.float32), -4.0, 4.0)
    return (noise_part * token_ramp).astype(jnp.bfloat16)


def level_of(rng, dims, shards, least, top_value):
    factor_of, own = 1.0, jax.random.fold_in(rng, 6)
    for position, shards_of in shards:
        steps = jnp.exp(jax.random.uniform(jax.random.fold_in(own, position), (shards_of,), jnp.float32, least / len(shards), top_value / len(shards)))
        factor_of = factor_of * jnp.repeat(steps, dims[position] // shards_of).reshape([-1 if axis == position else 1 for axis in range(len(dims))])
    return factor_of


def noise(key, extent, deviation, bound, cuts=(), kind=jnp.bfloat16):
    level = level_of(key, extent, cuts, -0.22, 0.18) if cuts else 1.0
    result = jax.random.normal(key, extent, jnp.float32) * deviation * level
    return jnp.minimum(jnp.maximum(result, -bound), bound).astype(kind)


def setup_inputs(seed: int = 0) -> dict:
    keys = jax.random.split(jax.random.key(seed), 8)
    query_rows = draw_query_rows(jax.random.fold_in(keys[7], 71), 0)
    key_rows = draw_key_rows(jax.random.fold_in(keys[7], 71), 0)
    value_rows = noise(keys[2], (CLIPS, SEQ_LEN, D), 1.0, 6.0, ((0, 2), (1, 16), (2, 8)))
    lengths = draw_lengths(jax.random.fold_in(keys[7], 71), 0)
    out_weight = noise(keys[4], (D, D), 0.7, 4.1875, ((0, 16), (1, 8)))
    gate_vector = jnp.clip(0.5 + 1.0 * jax.random.uniform(keys[5], (CLIPS, D), jnp.float32) ** level_of(keys[5], (CLIPS, D), ((0, 2),), -0.2, 0.2), 0.5, 1.5)
    cotangent = draw_cotangent(jax.random.fold_in(keys[7], 71), 0)
    return dict(query_rows=query_rows, key_rows=key_rows, value_rows=value_rows, lengths=lengths, out_weight=out_weight, gate_vector=gate_vector, cotangent=cotangent)


MASKED_SCORE = -1e+30

def to_heads(array):
    return array.reshape(CLIPS, SEQ_LEN, HEADS, HD).transpose(0, 2, 1, 3).reshape(CLIPS * HEADS, SEQ_LEN, HD)

def from_heads(array):
    return array.reshape(CLIPS, HEADS, SEQ_LEN, HD).transpose(0, 2, 1, 3).reshape(CLIPS, SEQ_LEN, D)

def head_forward(record):
    query_mat, key_mat, value_mat, length = record
    key_live = jnp.arange(SEQ_LEN) < length
    scores = jnp.dot(query_mat, key_mat.T, preferred_element_type=jnp.float32) * (1.0 / math.sqrt(HD))
    masked = jnp.where(key_live[None, :], scores, MASKED_SCORE)
    row_top = lax.optimization_barrier(jnp.max(masked, axis=1))
    weights = jnp.where(key_live[None, :], jnp.exp(masked - row_top[:, None]), 0.0)
    row_total = lax.optimization_barrier(jnp.sum(weights, axis=1))
    summed = jnp.dot(weights.astype(jnp.bfloat16), value_mat, preferred_element_type=jnp.float32)
    attended = (summed / row_total[:, None]).astype(jnp.bfloat16)
    return (attended, row_top + jnp.log(row_total))

def head_backward(record):
    query_mat, key_mat, value_mat, attended, grad_att, lse, length = record
    score_scale = 1.0 / math.sqrt(HD)
    key_live = jnp.arange(SEQ_LEN) < length
    scores = jnp.dot(query_mat, key_mat.T, preferred_element_type=jnp.float32) * score_scale
    probs = jnp.where(key_live[None, :], jnp.exp(scores - lse[:, None]), 0.0)
    row_delta = lax.optimization_barrier(jnp.sum(grad_att.astype(jnp.float32) * attended.astype(jnp.float32), axis=1))
    grad_probs = jnp.dot(grad_att, value_mat.T, preferred_element_type=jnp.float32)
    dscores = (probs * (grad_probs - row_delta[:, None]) * score_scale).astype(jnp.bfloat16)
    grad_value = jnp.dot(probs.astype(jnp.bfloat16).T, grad_att, preferred_element_type=jnp.float32).astype(jnp.bfloat16)
    grad_query = jnp.dot(dscores, key_mat, preferred_element_type=jnp.float32).astype(jnp.bfloat16)
    grad_key = jnp.dot(dscores.T, query_mat, preferred_element_type=jnp.float32).astype(jnp.bfloat16)
    return (grad_query, grad_key, grad_value)

def reference(query_rows, key_rows, value_rows, lengths, out_weight, gate_vector, cotangent):
    query_items = to_heads(query_rows)
    key_items = to_heads(key_rows)
    value_items = to_heads(value_rows)
    length_items = jnp.repeat(lengths, HEADS)
    attended_items, lse_items = lax.map(head_forward, (query_items, key_items, value_items, length_items))
    attended = from_heads(attended_items)

    def clip_step(running, record):
        clip_att, gate_row, cot_rows = record
        projected = jnp.dot(clip_att, out_weight.T, preferred_element_type=jnp.float32)
        branch = (gate_row[None, :] * projected).astype(jnp.bfloat16)
        gate_grad = lax.optimization_barrier(jnp.sum(cot_rows.astype(jnp.float32) * projected, axis=0))
        grad_proj = (gate_row[None, :] * cot_rows.astype(jnp.float32)).astype(jnp.bfloat16)
        grad_att = jnp.dot(grad_proj, out_weight, preferred_element_type=jnp.float32).astype(jnp.bfloat16)
        running = running + jnp.dot(grad_proj.T, clip_att, preferred_element_type=jnp.float32)
        return (running, (branch, gate_grad, grad_att))
    grad_weight, (branch_out, grad_gate, grad_attended) = lax.scan(clip_step, jnp.zeros((D, D), jnp.float32), (attended, gate_vector, cotangent))
    grad_items = lax.map(head_backward, (query_items, key_items, value_items, attended_items, to_heads(grad_attended), lse_items, length_items))
    grad_query = from_heads(grad_items[0])
    grad_key = from_heads(grad_items[1])
    grad_value = from_heads(grad_items[2])
    return (branch_out, grad_query, grad_key, grad_value, grad_weight, grad_gate)
```

```python
import functools
import math

import jax
import jax.numpy as jnp
from jax import lax
from jax.experimental import pallas as pl
from jax.experimental.pallas import tpu as pltpu
from jax.sharding import PartitionSpec as P

HD = 128
NX = 4
NY = 4
NZ = 4
MASKED = -1e30
MESH = pl.DeviceIdType.MESH
BF = jnp.bfloat16
F32 = jnp.float32


def dot_nn(a, b):
    return lax.dot_general(a, b, (((1,), (0,)), ((), ())), preferred_element_type=F32)


def dot_nt(a, b):
    return lax.dot_general(a, b, (((1,), (1,)), ((), ())), preferred_element_type=F32)


def dot_tn(a, b):
    return lax.dot_general(a, b, (((0,), (0,)), ((), ())), preferred_element_type=F32)


SEMS = {}
SEM_COUNT = 0
for sem_name, sem_size in (
    ("wa1", 3), ("wb1", 3), ("wa2", 3), ("wb2", 3), ("q", 3), ("k", 3), ("v", 3),
    ("gz", 3), ("gc", 1), ("gf", 3), ("o", 9), ("st", 3), ("do", 3), ("pc", 1), ("pz", 3),
    ("wx1", 3), ("wy1", 3), ("wx2", 3), ("wy2", 3), ("wd", 1), ("dl", 3),
    ("dk", 9), ("dv", 9), ("dq", 9), ("gx", 3), ("gy", 3),
):
    SEMS[sem_name] = SEM_COUNT
    SEM_COUNT += sem_size


def kernel(
    len_ref, q_ref, k_ref, v_ref, w_ref, gate_ref, cot_ref,
    br_ref, gq_ref, gk_ref, gv_ref, gw_ref, gg_ref,
    qbuf, kbuf, vbuf, gfull, wfull, scores, pbuf, top, stat, lse, wrow, wcol,
    osend, orecv, att, dobuf, dacc, psib, psrecv, pown, pzsend, pzrecv,
    dw, wxr, wyr, wxs, wys, wx2r, wy2r, wdsend, wdrecv, dls, delta,
    dks, dkr, dvs, dvr, dqs, dqr, dqacc, gxb, gyb,
    ss, rs,
):
    T = q_ref.shape[0]
    DL = q_ref.shape[1]
    NH = DL // HD
    Q = NX * T
    RA = T // 3
    scale = 1.0 / math.sqrt(HD)
    seq = lax.axis_index("seq")
    ten = lax.axis_index("tensor")
    dp = lax.axis_index("dp")
    x = lax.rem(seq, NX)
    y = lax.div(seq, NX)
    zh = lax.div(ten, 2)
    c = lax.rem(ten, 2)

    def xi(d):
        return lax.rem(x + d, NX)

    def yi(d):
        return lax.rem(y + d, NY)

    def zi(d):
        return lax.rem(zh + d, NZ)

    def X(d):
        return {"seq": y * NX + xi(d)}

    def Y(d):
        return {"seq": yi(d) * NX + x}

    def Z(d):
        return {"tensor": zi(d) * 2 + c}

    sibling = {"tensor": zh * 2 + 1 - c}
    twin = {"dp": 1 - dp}

    def rc(name, i, src, dst, peer):
        j = SEMS[name] + i
        return pltpu.make_async_remote_copy(
            src_ref=src, dst_ref=dst, send_sem=ss.at[j], recv_sem=rs.at[j],
            device_id=peer, device_id_type=MESH,
        )

    sent = []

    def go(*args):
        copy = rc(*args)
        copy.start()
        sent.append(copy)
        return copy

    def lanes(h):
        return pl.ds(pl.multiple_of(h * HD, HD), HD)

    barrier = pltpu.get_barrier_semaphore()
    peers = [X(d) for d in (1, 2, 3)] + [Y(d) for d in (1, 2, 3)] + [Z(d) for d in (1, 2, 3)]
    peers += [sibling, twin]
    for peer in peers:
        pl.semaphore_signal(barrier, inc=1, device_id=peer, device_id_type=MESH)
    gate_local = gate_ref[:, pl.ds(pl.multiple_of(ten * DL, HD), DL)]
    gfull[ten] = (gate_local * cot_ref[...].astype(F32)).astype(BF)
    qbuf[x] = q_ref[...]
    kbuf[y] = k_ref[...]
    vbuf[y] = v_ref[...]
    wfull[y, x] = w_ref[...]
    wrow[...] = jnp.zeros_like(wrow)
    pl.semaphore_wait(barrier, len(peers))

    wa1 = [go("wa1", d - 1, w_ref.at[0:RA], wfull.at[y, x, 0:RA], X(d)) for d in (1, 2, 3)]
    wb1 = [go("wb1", d - 1, w_ref.at[RA:T], wfull.at[y, x, RA:T], Y(d)) for d in (1, 2, 3)]
    q_in = [go("q", d - 1, q_ref, qbuf.at[x], X(d)) for d in (1, 2, 3)]
    k_in = [go("k", d - 1, k_ref, kbuf.at[y], Y(d)) for d in (1, 2, 3)]
    v_in = [go("v", d - 1, v_ref, vbuf.at[y], Y(d)) for d in (1, 2, 3)]
    g_in = [go("gz", d - 1, gfull.at[ten], gfull.at[ten], Z(d)) for d in (1, 2, 3)]
    g_sib = go("gc", 0, gfull.at[ten], gfull.at[ten], sibling)

    for copy in wa1:
        copy.wait_recv()
    wa2 = [go("wa2", d - 1, wfull.at[y, :, 0:RA], wfull.at[y, :, 0:RA], Y(d)) for d in (1, 2, 3)]
    for copy in wb1:
        copy.wait_recv()
    wb2 = [go("wb2", d - 1, wfull.at[:, x, RA:T], wfull.at[:, x, RA:T], X(d)) for d in (1, 2, 3)]

    for copy in q_in:
        copy.wait_recv()
    length = len_ref[0]
    top[...] = jnp.full_like(top, MASKED)

    def score_block(j):
        rows = (j * NX + x) * T + lax.broadcasted_iota(jnp.int32, (T, 1), 0)
        live = rows < length

        def head(h, carry):
            s = dot_nt(kbuf[j, :, lanes(h)], qbuf[:, :, lanes(h)].reshape(Q, HD)) * scale
            s = jnp.where(live, s, MASKED)
            scores[h, j] = s
            top[pl.ds(h, 1), :] = jnp.maximum(
                top[pl.ds(h, 1), :], jnp.max(s, axis=0, keepdims=True)
            )
            return carry

        lax.fori_loop(0, NH, head, 0)

    score_block(y)
    for d in (3, 1, 2):
        k_in[d - 1].wait_recv()
        score_block(yi(NY - d))

    g_fwd = []
    for d in (1, 3, 2):
        g_in[d - 1].wait_recv()
        t = zi(NZ - d) * 2 + c
        g_fwd.append(go("gf", d - 1, gfull.at[t], gfull.at[t], sibling))

    for copy in v_in:
        copy.wait_recv()

    stat[x] = jnp.zeros((8, Q), F32)

    def forward_head(h, carry):
        row_top = top[pl.ds(h, 1), :]

        def block(j, total):
            p = jnp.exp(scores[h, j] - row_top)
            pbuf[j] = p.astype(BF)
            return total + jnp.sum(p, axis=0, keepdims=True)

        total = lax.fori_loop(0, NY, block, jnp.zeros((1, Q), F32))
        out_t = dot_tn(vbuf[:, :, lanes(h)].reshape(Q, HD), pbuf[...].reshape(Q, Q))
        out_t = out_t / total
        osend[:, :, lanes(h)] = out_t.T.astype(BF).reshape(NX, T, HD)
        stat[x, pl.ds(h, 1), :] = row_top + jnp.log(total)
        for d in (1, 2, 3):
            rc(
                "o", h * 3 + d - 1, osend.at[xi(d), :, lanes(h)],
                orecv.at[x, :, lanes(h)], X(d),
            ).start()
        return carry

    lax.fori_loop(0, NH, forward_head, 0)
    st_in = [go("st", d - 1, stat.at[x], stat.at[x], X(d)) for d in (1, 2, 3)]
    orecv[x] = osend[x]

    for copy in wa2 + wb2 + g_fwd + [g_sib]:
        copy.wait_recv()

    def weight_rows(t):
        return wfull[lax.div(t, 2), pl.ds(lax.rem(t, 2) * 2, 2)].reshape(2 * T, DL)

    dacc[...] = jnp.zeros_like(dacc)

    def grad_step(t, carry):
        dacc[...] += dot_nn(gfull[t], weight_rows(t))
        return carry

    lax.fori_loop(0, 2 * NZ, grad_step, 0)
    dobuf[x] = dacc[...].astype(BF)
    do_in = [go("do", d - 1, dobuf.at[x], dobuf.at[x], X(d)) for d in (1, 2, 3)]

    for copy in st_in:
        copy.wait_recv()
    for h in range(NH):
        parts = [stat[j, h : h + 1, :] for j in range(NX)]
        high = functools.reduce(jnp.maximum, parts)
        row_lse = high + jnp.log(sum(jnp.exp(part - high) for part in parts))
        lse[h : h + 1, :] = row_lse
        for j in range(NX):
            wrow[h * NX + j : h * NX + j + 1, :] = jnp.exp(parts[j] - row_lse)
    wcol[...] = wrow[...].T

    def o_copy(h, d):
        return rc(
            "o", h * 3 + d - 1, osend.at[xi(d), :, lanes(h)], orecv.at[x, :, lanes(h)], X(d)
        )

    def wait_o(h, carry):
        for d in (1, 2, 3):
            o_copy(h, d).wait_recv()
        return carry

    lax.fori_loop(0, NH, wait_o, 0)
    weights = wcol[pl.ds(pl.multiple_of(x * T, 64), T), :]
    for h in range(NH):
        total = jnp.zeros((T, HD), F32)
        for j in range(NX):
            col = h * NX + j
            total += weights[:, col : col + 1] * orecv[j, :, h * HD : (h + 1) * HD].astype(F32)
        att[:, h * HD : (h + 1) * HD] = total.astype(BF)

    def proj_sib(z, carry):
        rows = wfull[z, pl.ds((1 - c) * 2, 2)].reshape(2 * T, DL)
        psib[z] = dot_nt(att[...], rows).astype(BF)
        return carry

    lax.fori_loop(0, NZ, proj_sib, 0)
    p_sib = go("pc", 0, psib, psrecv, sibling)

    def weight_grad(t, carry):
        part = dot_tn(gfull[t], att[...]).astype(BF).reshape(2, T, DL)
        dw[lax.div(t, 2), pl.ds(lax.rem(t, 2) * 2, 2)] = part
        return carry

    lax.fori_loop(0, 2 * NZ, weight_grad, 0)
    wx1 = [go("wx1", d - 1, dw.at[:, xi(d), 0:RA], wxr.at[d - 1], X(d)) for d in (1, 2, 3)]
    wy1 = [go("wy1", d - 1, dw.at[yi(d), :, RA:T], wyr.at[d - 1], Y(d)) for d in (1, 2, 3)]

    def proj_own(z, carry):
        rows = wfull[z, pl.ds(c * 2, 2)].reshape(2 * T, DL)
        pown[z] = dot_nt(att[...], rows)
        return carry

    lax.fori_loop(0, NZ, proj_own, 0)
    p_sib.wait_recv()

    def proj_add(z, carry):
        value = pown[z] + psrecv[z].astype(F32)
        pown[z] = value
        pzsend[z] = value.astype(BF)
        return carry

    lax.fori_loop(0, NZ, proj_add, 0)
    pz = [go("pz", d - 1, pzsend.at[zi(d)], pzrecv.at[d - 1], Z(d)) for d in (1, 2, 3)]

    for copy in do_in:
        copy.wait_recv()
    ones = jnp.ones((8, HD), F32)
    dls[x] = jnp.zeros((8, Q), F32)
    for h in range(NH):
        sl = slice(h * HD, (h + 1) * HD)
        prod = dobuf[:, :, sl].astype(F32) * osend[:, :, sl].astype(F32)
        rows = lax.dot_general(
            ones, prod.reshape(Q, HD), (((1,), (1,)), ((), ())),
            preferred_element_type=F32, precision=lax.Precision.HIGHEST,
        )
        dls[x, h : h + 1, :] = rows[0:1, :]
    dl_in = [go("dl", d - 1, dls.at[x], dls.at[x], X(d)) for d in (1, 2, 3)]
    for copy in dl_in:
        copy.wait_recv()
    for h in range(NH):
        delta[h : h + 1, :] = sum(
            wrow[h * NX + j : h * NX + j + 1, :] * dls[j, h : h + 1, :] for j in range(NX)
        )

    def kv_copy(name, h, d, src, dst):
        return rc(
            name, h * 3 + d - 1, src.at[yi(d), :, lanes(h)], dst.at[d - 1, :, lanes(h)], Y(d)
        )

    def q_copy(h, d):
        return rc("dq", h * 3 + d - 1, dqs.at[xi(d), :, lanes(h)], dqr.at[d - 1, :, lanes(h)], X(d))

    def backward_head(h, carry):
        row_lse = lse[pl.ds(h, 1), :]
        row_delta = delta[pl.ds(h, 1), :]
        dqacc[...] = jnp.zeros_like(dqacc)
        for d in (1, 2, 3, 0):
            j = yi(d)
            grads = dobuf[:, :, lanes(h)].reshape(Q, HD)
            p = jnp.exp(scores[h, j] - row_lse)
            dp_t = dot_nt(vbuf[j, :, lanes(h)], grads)
            ds = (p * (dp_t - row_delta) * scale).astype(BF)
            dvs[j, :, lanes(h)] = dot_nn(p.astype(BF), grads).astype(BF)
            dks[j, :, lanes(h)] = dot_nn(ds, qbuf[:, :, lanes(h)].reshape(Q, HD)).astype(BF)
            if d:
                kv_copy("dv", h, d, dvs, dvr).start()
                kv_copy("dk", h, d, dks, dkr).start()
            dqacc[...] += dot_tn(kbuf[j, :, lanes(h)], ds)
        dqs[:, :, lanes(h)] = dqacc[...].T.astype(BF).reshape(NX, T, HD)
        for d in (1, 2, 3):
            q_copy(h, d).start()
        return carry

    lax.fori_loop(0, NH, backward_head, 0)

    for copy in wx1:
        copy.wait_recv()

    def sum_x(j, carry):
        total = dw[j, x, 0:RA].astype(F32)
        for d in (1, 2, 3):
            total += wxr[d - 1, j].astype(F32)
        wxs[j] = total.astype(BF)
        return carry

    lax.fori_loop(0, NY, sum_x, 0)
    wx2 = [go("wx2", d - 1, wxs.at[yi(d)], wx2r.at[d - 1], Y(d)) for d in (1, 2, 3)]
    for copy in wy1:
        copy.wait_recv()

    def sum_y(j, carry):
        total = dw[y, j, RA:T].astype(F32)
        for d in (1, 2, 3):
            total += wyr[d - 1, j].astype(F32)
        wys[j] = total.astype(BF)
        return carry

    lax.fori_loop(0, NX, sum_y, 0)
    wy2 = [go("wy2", d - 1, wys.at[xi(d)], wy2r.at[d - 1], X(d)) for d in (1, 2, 3)]

    for copy in pz:
        copy.wait_recv()
    projected = pown[zh]
    for d in (1, 2, 3):
        projected += pzrecv[d - 1].astype(F32)
    br_ref[...] = (gate_local * projected).astype(BF)
    gxb[x] = jnp.broadcast_to(
        jnp.sum(cot_ref[...].astype(F32) * projected, axis=0, keepdims=True), (8, DL)
    )
    gx = [go("gx", d - 1, gxb.at[x], gxb.at[x], X(d)) for d in (1, 2, 3)]

    for copy in wx2 + wy2:
        copy.wait_recv()
    total_a = wxs[y].astype(F32)
    total_b = wys[x].astype(F32)
    for d in (1, 2, 3):
        total_a += wx2r[d - 1].astype(F32)
        total_b += wy2r[d - 1].astype(F32)
    wdsend[0:RA] = total_a.astype(BF)
    wdsend[RA:T] = total_b.astype(BF)
    wd = go("wd", 0, wdsend, wdrecv, twin)

    for copy in gx:
        copy.wait_recv()
    gyb[y] = gxb[0] + gxb[1] + gxb[2] + gxb[3]
    gy = [go("gy", d - 1, gyb.at[y], gyb.at[y], Y(d)) for d in (1, 2, 3)]

    def wait_grads(h, carry):
        for d in (1, 2, 3):
            kv_copy("dv", h, d, dvs, dvr).wait_recv()
            kv_copy("dk", h, d, dks, dkr).wait_recv()
            q_copy(h, d).wait_recv()
        return carry

    lax.fori_loop(0, NH, wait_grads, 0)
    for out, own, got, index in ((gv_ref, dvs, dvr, y), (gk_ref, dks, dkr, y), (gq_ref, dqs, dqr, x)):
        total = own[index].astype(F32)
        for d in (1, 2, 3):
            total += got[d - 1].astype(F32)
        out[...] = total.astype(BF)

    wd.wait_recv()
    gw_ref[...] = wdsend[...].astype(F32) + wdrecv[...].astype(F32)
    for copy in gy:
        copy.wait_recv()
    gg_ref[...] = (gyb[0] + gyb[1] + gyb[2] + gyb[3])[0:1, :]

    def wait_sends(h, carry):
        for d in (1, 2, 3):
            o_copy(h, d).wait_send()
            kv_copy("dv", h, d, dvs, dvr).wait_send()
            kv_copy("dk", h, d, dks, dkr).wait_send()
            q_copy(h, d).wait_send()
        return carry

    lax.fori_loop(0, NH, wait_sends, 0)
    for copy in sent:
        copy.wait_send()


def shards(query_rows, key_rows, value_rows, lengths, out_weight, gate_vector, cotangent):
    T, DL = query_rows.shape[1:]
    NH = DL // HD
    Q = NX * T
    RA = T // 3
    D = gate_vector.shape[1]

    def vm(shape, dtype=BF):
        return pltpu.VMEM(shape, dtype)

    blocks = (4, T, DL)
    three = (3, T, DL)
    scratch = [
        vm(blocks), vm(blocks), vm(blocks), vm((2 * NZ, T, DL)), vm((NY, NX, T, DL)),
        vm((NH, NY, T, Q), F32), vm((NY, T, Q)), vm((8, Q), F32), vm((NX, 8, Q), F32),
        vm((8, Q), F32), vm((HD, Q), F32), vm((Q, HD), F32),
        vm(blocks), vm(blocks), vm((T, DL)), vm(blocks), vm((T, DL), F32),
        vm(blocks), vm(blocks), vm(blocks, F32), vm(blocks), vm(three),
        vm((NY, NX, T, DL)), vm((3, NY, RA, DL)), vm((3, NX, T - RA, DL)),
        vm((NY, RA, DL)), vm((NX, T - RA, DL)), vm((3, RA, DL)), vm((3, T - RA, DL)),
        vm((T, DL)), vm((T, DL)), vm((NX, 8, Q), F32), vm((8, Q), F32),
        vm(blocks), vm(three), vm(blocks), vm(three), vm(blocks), vm(three), vm((HD, Q), F32),
        vm((NX, 8, DL), F32), vm((NY, 8, DL), F32),
        pltpu.SemaphoreType.DMA((SEM_COUNT,)), pltpu.SemaphoreType.DMA((SEM_COUNT,)),
    ]
    vmem = pl.BlockSpec(memory_space=pltpu.VMEM)
    rows = jax.ShapeDtypeStruct((T, DL), BF)
    outs = pl.pallas_call(
        kernel,
        out_shape=(
            rows, rows, rows, rows,
            jax.ShapeDtypeStruct((T, DL), F32),
            jax.ShapeDtypeStruct((1, DL), F32),
        ),
        in_specs=[pl.BlockSpec(memory_space=pltpu.SMEM)] + [vmem] * 6,
        out_specs=(vmem,) * 6,
        scratch_shapes=scratch,
        compiler_params=pltpu.CompilerParams(
            collective_id=0, has_side_effects=True, vmem_limit_bytes=60 * 1024 * 1024
        ),
    )(lengths, query_rows[0], key_rows[0], value_rows[0], out_weight, gate_vector, cotangent[0])
    branch, grad_q, grad_k, grad_v, grad_w, grad_g = outs
    return branch[None], grad_q[None], grad_k[None], grad_v[None], grad_w, grad_g


def solution(mesh):
    rows = P("dp", "seq", "tensor")
    placed = (rows, rows, rows, P("dp"), P("seq", "tensor"), P("dp", None), rows)
    return jax.shard_map(
        shards,
        mesh=mesh,
        in_specs=placed,
        out_specs=(rows, rows, rows, rows, P("seq", "tensor"), P("dp", "tensor")),
        check_vma=False,
    )
```

```python
import functools
import math

import jax
import jax.numpy as jnp
from jax import lax
from jax.experimental import pallas as pl
from jax.experimental.pallas import tpu as pltpu
from jax.sharding import PartitionSpec as P

HD = 128
NX = 4
NY = 4
NZ = 4
MASKED = -1e30
MESH = pl.DeviceIdType.MESH
BF = jnp.bfloat16
F32 = jnp.float32


def dot_nn(a, b):
    return lax.dot_general(a, b, (((1,), (0,)), ((), ())), preferred_element_type=F32)


def dot_nt(a, b):
    return lax.dot_general(a, b, (((1,), (1,)), ((), ())), preferred_element_type=F32)


def dot_tn(a, b):
    return lax.dot_general(a, b, (((0,), (0,)), ((), ())), preferred_element_type=F32)


SEMS = {}
SEM_COUNT = 0
for sem_name, sem_size in (
    ("wa1", 3), ("wb1", 3), ("wa2", 3), ("wb2", 3), ("q", 3), ("k", 3), ("v", 3),
    ("gz", 3), ("gc", 1), ("gf", 3), ("o", 9), ("st", 3), ("do", 3), ("pc", 1), ("pz", 3),
    ("wx1", 3), ("wy1", 3), ("wx2", 3), ("wy2", 3), ("wd", 1), ("dl", 3),
    ("dk", 9), ("dv", 9), ("dq", 9), ("gx", 3), ("gy", 3),
):
    SEMS[sem_name] = SEM_COUNT
    SEM_COUNT += sem_size


def kernel(
    len_ref, q_ref, k_ref, v_ref, w_ref, gate_ref, cot_ref,
    br_ref, gq_ref, gk_ref, gv_ref, gw_ref, gg_ref,
    qbuf, kbuf, vbuf, gfull, wfull, scores, pbuf, top, stat, lse, wrow, wcol,
    osend, orecv, att, dobuf, dacc, psib, psrecv, pown, pzsend, pzrecv,
    dw, wxr, wyr, wxs, wys, wx2r, wy2r, wdsend, wdrecv, dls, delta,
    dks, dkr, dvs, dvr, dqs, dqr, dqacc, gxb, gyb,
    ss, rs,
):
    T = q_ref.shape[0]
    DL = q_ref.shape[1]
    NH = DL // HD
    Q = NX * T
    RA = T // 2
    scale = 1.0 / math.sqrt(HD)
    seq = lax.axis_index("seq")
    ten = lax.axis_index("tensor")
    dp = lax.axis_index("dp")
    x = lax.rem(seq, NX)
    y = lax.div(seq, NX)
    zh = lax.div(ten, 2)
    c = lax.rem(ten, 2)

    def xi(d):
        return lax.rem(x + d, NX)

    def yi(d):
        return lax.rem(y + d, NY)

    def zi(d):
        return lax.rem(zh + d, NZ)

    def X(d):
        return {"seq": y * NX + xi(d)}

    def Y(d):
        return {"seq": yi(d) * NX + x}

    def Z(d):
        return {"tensor": zi(d) * 2 + c}

    sibling = {"tensor": zh * 2 + 1 - c}
    twin = {"dp": 1 - dp}

    def rc(name, i, src, dst, peer):
        j = SEMS[name] + i
        return pltpu.make_async_remote_copy(
            src_ref=src, dst_ref=dst, send_sem=ss.at[j], recv_sem=rs.at[j],
            device_id=peer, device_id_type=MESH,
        )

    sent = []

    def go(*args):
        copy = rc(*args)
        copy.start()
        sent.append(copy)
        return copy

    def lanes(h):
        return pl.ds(pl.multiple_of(h * HD, HD), HD)

    barrier = pltpu.get_barrier_semaphore()
    peers = [X(d) for d in (1, 2, 3)] + [Y(d) for d in (1, 2, 3)] + [Z(d) for d in (1, 2, 3)]
    peers += [sibling, twin]
    for peer in peers:
        pl.semaphore_signal(barrier, inc=1, device_id=peer, device_id_type=MESH)
    gate_local = gate_ref[:, pl.ds(pl.multiple_of(ten * DL, HD), DL)]
    gfull[ten] = (gate_local * cot_ref[...].astype(F32)).astype(BF)
    qbuf[x] = q_ref[...]
    kbuf[y] = k_ref[...]
    vbuf[y] = v_ref[...]
    wfull[y, x] = w_ref[...]
    wrow[...] = jnp.zeros_like(wrow)
    pl.semaphore_wait(barrier, len(peers))

    wa1 = [go("wa1", d - 1, w_ref.at[0:RA], wfull.at[y, x, 0:RA], X(d)) for d in (1, 2, 3)]
    wb1 = [go("wb1", d - 1, w_ref.at[RA:T], wfull.at[y, x, RA:T], Y(d)) for d in (1, 2, 3)]
    q_in = [go("q", d - 1, q_ref, qbuf.at[x], X(d)) for d in (1, 2, 3)]
    k_in = [go("k", d - 1, k_ref, kbuf.at[y], Y(d)) for d in (1, 2, 3)]
    v_in = [go("v", d - 1, v_ref, vbuf.at[y], Y(d)) for d in (1, 2, 3)]
    g_in = [go("gz", d - 1, gfull.at[ten], gfull.at[ten], Z(d)) for d in (1, 2, 3)]
    g_sib = go("gc", 0, gfull.at[ten], gfull.at[ten], sibling)

    for copy in wa1:
        copy.wait_recv()
    wa2 = [go("wa2", d - 1, wfull.at[y, :, 0:RA], wfull.at[y, :, 0:RA], Y(d)) for d in (1, 2, 3)]
    for copy in wb1:
        copy.wait_recv()
    wb2 = [go("wb2", d - 1, wfull.at[:, x, RA:T], wfull.at[:, x, RA:T], X(d)) for d in (1, 2, 3)]

    for copy in q_in:
        copy.wait_recv()
    length = len_ref[0]
    top[...] = jnp.full_like(top, MASKED)

    def score_block(j):
        rows = (j * NX + x) * T + lax.broadcasted_iota(jnp.int32, (T, 1), 0)
        live = rows < length

        def head(h, carry):
            s = dot_nt(kbuf[j, :, lanes(h)], qbuf[:, :, lanes(h)].reshape(Q, HD)) * scale
            s = jnp.where(live, s, MASKED)
            scores[h, j] = s
            top[pl.ds(h, 1), :] = jnp.maximum(
                top[pl.ds(h, 1), :], jnp.max(s, axis=0, keepdims=True)
            )
            return carry

        lax.fori_loop(0, NH, head, 0)

    score_block(y)
    for d in (3, 1, 2):
        k_in[d - 1].wait_recv()
        score_block(yi(NY - d))

    g_fwd = []
    for d in (1, 3, 2):
        g_in[d - 1].wait_recv()
        t = zi(NZ - d) * 2 + c
        g_fwd.append(go("gf", d - 1, gfull.at[t], gfull.at[t], sibling))

    for copy in v_in:
        copy.wait_recv()

    stat[x] = jnp.zeros((8, Q), F32)

    def forward_head(h, carry):
        row_top = top[pl.ds(h, 1), :]

        def block(j, total):
            p = jnp.exp(scores[h, j] - row_top)
            pbuf[j] = p.astype(BF)
            return total + jnp.sum(p, axis=0, keepdims=True)

        total = lax.fori_loop(0, NY, block, jnp.zeros((1, Q), F32))
        out_t = dot_tn(vbuf[:, :, lanes(h)].reshape(Q, HD), pbuf[...].reshape(Q, Q))
        out_t = out_t / total
        osend[:, :, lanes(h)] = out_t.T.astype(BF).reshape(NX, T, HD)
        stat[x, pl.ds(h, 1), :] = row_top + jnp.log(total)
        for d in (1, 2, 3):
            rc(
                "o", h * 3 + d - 1, osend.at[xi(d), :, lanes(h)],
                orecv.at[x, :, lanes(h)], X(d),
            ).start()
        return carry

    lax.fori_loop(0, NH, forward_head, 0)
    st_in = [go("st", d - 1, stat.at[x], stat.at[x], X(d)) for d in (1, 2, 3)]
    orecv[x] = osend[x]

    for copy in wa2 + wb2 + g_fwd + [g_sib]:
        copy.wait_recv()

    def weight_rows(t):
        return wfull[lax.div(t, 2), pl.ds(lax.rem(t, 2) * 2, 2)].reshape(2 * T, DL)

    dacc[...] = jnp.zeros_like(dacc)

    def grad_step(t, carry):
        dacc[...] += dot_nn(gfull[t], weight_rows(t))
        return carry

    lax.fori_loop(0, 2 * NZ, grad_step, 0)
    dobuf[x] = dacc[...].astype(BF)
    do_in = [go("do", d - 1, dobuf.at[x], dobuf.at[x], X(d)) for d in (1, 2, 3)]

    for copy in st_in:
        copy.wait_recv()
    for h in range(NH):
        parts = [stat[j, h : h + 1, :] for j in range(NX)]
        high = functools.reduce(jnp.maximum, parts)
        row_lse = high + jnp.log(sum(jnp.exp(part - high) for part in parts))
        lse[h : h + 1, :] = row_lse
        for j in range(NX):
            wrow[h * NX + j : h * NX + j + 1, :] = jnp.exp(parts[j] - row_lse)
    wcol[...] = wrow[...].T

    def o_copy(h, d):
        return rc(
            "o", h * 3 + d - 1, osend.at[xi(d), :, lanes(h)], orecv.at[x, :, lanes(h)], X(d)
        )

    def wait_o(h, carry):
        for d in (1, 2, 3):
            o_copy(h, d).wait_recv()
        return carry

    lax.fori_loop(0, NH, wait_o, 0)
    weights = wcol[pl.ds(pl.multiple_of(x * T, 64), T), :]
    for h in range(NH):
        total = jnp.zeros((T, HD), F32)
        for j in range(NX):
            col = h * NX + j
            total += weights[:, col : col + 1] * orecv[j, :, h * HD : (h + 1) * HD].astype(F32)
        att[:, h * HD : (h + 1) * HD] = total.astype(BF)

    def proj_sib(z, carry):
        rows = wfull[z, pl.ds((1 - c) * 2, 2)].reshape(2 * T, DL)
        psib[z] = dot_nt(att[...], rows).astype(BF)
        return carry

    lax.fori_loop(0, NZ, proj_sib, 0)
    p_sib = go("pc", 0, psib, psrecv, sibling)

    def weight_grad(t, carry):
        part = dot_tn(gfull[t], att[...]).astype(BF).reshape(2, T, DL)
        dw[lax.div(t, 2), pl.ds(lax.rem(t, 2) * 2, 2)] = part
        return carry

    lax.fori_loop(0, 2 * NZ, weight_grad, 0)
    wx1 = [go("wx1", d - 1, dw.at[:, xi(d), 0:RA], wxr.at[d - 1], X(d)) for d in (1, 2, 3)]
    wy1 = [go("wy1", d - 1, dw.at[yi(d), :, RA:T], wyr.at[d - 1], Y(d)) for d in (1, 2, 3)]

    def proj_own(z, carry):
        rows = wfull[z, pl.ds(c * 2, 2)].reshape(2 * T, DL)
        pown[z] = dot_nt(att[...], rows)
        return carry

    lax.fori_loop(0, NZ, proj_own, 0)
    p_sib.wait_recv()

    def proj_add(z, carry):
        value = pown[z] + psrecv[z].astype(F32)
        pown[z] = value
        pzsend[z] = value.astype(BF)
        return carry

    lax.fori_loop(0, NZ, proj_add, 0)
    pz = [go("pz", d - 1, pzsend.at[zi(d)], pzrecv.at[d - 1], Z(d)) for d in (1, 2, 3)]

    for copy in do_in:
        copy.wait_recv()
    ones = jnp.ones((8, HD), F32)
    dls[x] = jnp.zeros((8, Q), F32)
    for h in range(NH):
        sl = slice(h * HD, (h + 1) * HD)
        prod = dobuf[:, :, sl].astype(F32) * osend[:, :, sl].astype(F32)
        rows = lax.dot_general(
            ones, prod.reshape(Q, HD), (((1,), (1,)), ((), ())),
            preferred_element_type=F32, precision=lax.Precision.HIGHEST,
        )
        dls[x, h : h + 1, :] = rows[0:1, :]
    dl_in = [go("dl", d - 1, dls.at[x], dls.at[x], X(d)) for d in (1, 2, 3)]
    for copy in dl_in:
        copy.wait_recv()
    for h in range(NH):
        delta[h : h + 1, :] = sum(
            wrow[h * NX + j : h * NX + j + 1, :] * dls[j, h : h + 1, :] for j in range(NX)
        )

    def kv_copy(name, h, d, src, dst):
        return rc(
            name, h * 3 + d - 1, src.at[yi(d), :, lanes(h)], dst.at[d - 1, :, lanes(h)], Y(d)
        )

    def q_copy(h, d):
        return rc("dq", h * 3 + d - 1, dqs.at[xi(d), :, lanes(h)], dqr.at[d - 1, :, lanes(h)], X(d))

    def backward_head(h, carry):
        row_lse = lse[pl.ds(h, 1), :]
        row_delta = delta[pl.ds(h, 1), :]
        dqacc[...] = jnp.zeros_like(dqacc)
        for d in (1, 2, 3, 0):
            j = yi(d)
            grads = dobuf[:, :, lanes(h)].reshape(Q, HD)
            p = jnp.exp(scores[h, j] - row_lse)
            dp_t = dot_nt(vbuf[j, :, lanes(h)], grads)
            ds = (p * (dp_t - row_delta) * scale).astype(BF)
            dvs[j, :, lanes(h)] = dot_nn(p.astype(BF), grads).astype(BF)
            dks[j, :, lanes(h)] = dot_nn(ds, qbuf[:, :, lanes(h)].reshape(Q, HD)).astype(BF)
            if d:
                kv_copy("dv", h, d, dvs, dvr).start()
                kv_copy("dk", h, d, dks, dkr).start()
            dqacc[...] += dot_tn(kbuf[j, :, lanes(h)], ds)
        dqs[:, :, lanes(h)] = dqacc[...].T.astype(BF).reshape(NX, T, HD)
        for d in (1, 2, 3):
            q_copy(h, d).start()
        return carry

    lax.fori_loop(0, NH, backward_head, 0)

    for copy in wx1:
        copy.wait_recv()

    def sum_x(j, carry):
        total = dw[j, x, 0:RA].astype(F32)
        for d in (1, 2, 3):
            total += wxr[d - 1, j].astype(F32)
        wxs[j] = total.astype(BF)
        return carry

    lax.fori_loop(0, NY, sum_x, 0)
    wx2 = [go("wx2", d - 1, wxs.at[yi(d)], wx2r.at[d - 1], Y(d)) for d in (1, 2, 3)]
    for copy in wy1:
        copy.wait_recv()

    def sum_y(j, carry):
        total = dw[y, j, RA:T].astype(F32)
        for d in (1, 2, 3):
            total += wyr[d - 1, j].astype(F32)
        wys[j] = total.astype(BF)
        return carry

    lax.fori_loop(0, NX, sum_y, 0)
    wy2 = [go("wy2", d - 1, wys.at[xi(d)], wy2r.at[d - 1], X(d)) for d in (1, 2, 3)]

    for copy in pz:
        copy.wait_recv()
    projected = pown[zh]
    for d in (1, 2, 3):
        projected += pzrecv[d - 1].astype(F32)
    br_ref[...] = (gate_local * projected).astype(BF)
    gxb[x] = jnp.broadcast_to(
        jnp.sum(cot_ref[...].astype(F32) * projected, axis=0, keepdims=True), (8, DL)
    )
    gx = [go("gx", d - 1, gxb.at[x], gxb.at[x], X(d)) for d in (1, 2, 3)]

    for copy in wx2 + wy2:
        copy.wait_recv()
    total_a = wxs[y].astype(F32)
    total_b = wys[x].astype(F32)
    for d in (1, 2, 3):
        total_a += wx2r[d - 1].astype(F32)
        total_b += wy2r[d - 1].astype(F32)
    wdsend[0:RA] = total_a.astype(BF)
    wdsend[RA:T] = total_b.astype(BF)
    wd = go("wd", 0, wdsend, wdrecv, twin)

    for copy in gx:
        copy.wait_recv()
    gyb[y] = gxb[0] + gxb[1] + gxb[2] + gxb[3]
    gy = [go("gy", d - 1, gyb.at[y], gyb.at[y], Y(d)) for d in (1, 2, 3)]

    def wait_grads(h, carry):
        for d in (1, 2, 3):
            kv_copy("dv", h, d, dvs, dvr).wait_recv()
            kv_copy("dk", h, d, dks, dkr).wait_recv()
            q_copy(h, d).wait_recv()
        return carry

    lax.fori_loop(0, NH, wait_grads, 0)
    for out, own, got, index in ((gv_ref, dvs, dvr, y), (gk_ref, dks, dkr, y), (gq_ref, dqs, dqr, x)):
        total = own[index].astype(F32)
        for d in (1, 2, 3):
            total += got[d - 1].astype(F32)
        out[...] = total.astype(BF)

    wd.wait_recv()
    gw_ref[...] = wdsend[...].astype(F32) + wdrecv[...].astype(F32)
    for copy in gy:
        copy.wait_recv()
    gg_ref[...] = (gyb[0] + gyb[1] + gyb[2] + gyb[3])[0:1, :]

    def wait_sends(h, carry):
        for d in (1, 2, 3):
            o_copy(h, d).wait_send()
            kv_copy("dv", h, d, dvs, dvr).wait_send()
            kv_copy("dk", h, d, dks, dkr).wait_send()
            q_copy(h, d).wait_send()
        return carry

    lax.fori_loop(0, NH, wait_sends, 0)
    for copy in sent:
        copy.wait_send()


def place(*refs):
    for i in range(6):
        refs[6 + i][...] = refs[i][...]


def shards(query_rows, key_rows, value_rows, lengths, out_weight, gate_vector, cotangent):
    T, DL = query_rows.shape[1:]
    NH = DL // HD
    Q = NX * T
    RA = T // 2
    D = gate_vector.shape[1]

    def vm(shape, dtype=BF):
        return pltpu.VMEM(shape, dtype)

    blocks = (4, T, DL)
    three = (3, T, DL)
    scratch = [
        vm(blocks), vm(blocks), vm(blocks), vm((2 * NZ, T, DL)), vm((NY, NX, T, DL)),
        vm((NH, NY, T, Q), F32), vm((NY, T, Q)), vm((8, Q), F32), vm((NX, 8, Q), F32),
        vm((8, Q), F32), vm((HD, Q), F32), vm((Q, HD), F32),
        vm(blocks), vm(blocks), vm((T, DL)), vm(blocks), vm((T, DL), F32),
        vm(blocks), vm(blocks), vm(blocks, F32), vm(blocks), vm(three),
        vm((NY, NX, T, DL)), vm((3, NY, RA, DL)), vm((3, NX, T - RA, DL)),
        vm((NY, RA, DL)), vm((NX, T - RA, DL)), vm((3, RA, DL)), vm((3, T - RA, DL)),
        vm((T, DL)), vm((T, DL)), vm((NX, 8, Q), F32), vm((8, Q), F32),
        vm(blocks), vm(three), vm(blocks), vm(three), vm(blocks), vm(three), vm((HD, Q), F32),
        vm((NX, 8, DL), F32), vm((NY, 8, DL), F32),
        pltpu.SemaphoreType.DMA((SEM_COUNT,)), pltpu.SemaphoreType.DMA((SEM_COUNT,)),
    ]
    vmem = pl.BlockSpec(memory_space=pltpu.VMEM)
    rows = jax.ShapeDtypeStruct((T, DL), BF)
    outs = pl.pallas_call(
        kernel,
        out_shape=(
            rows, rows, rows, rows,
            jax.ShapeDtypeStruct((T, DL), F32),
            jax.ShapeDtypeStruct((1, DL), F32),
        ),
        in_specs=[pl.BlockSpec(memory_space=pltpu.SMEM)] + [vmem] * 6,
        out_specs=(vmem,) * 6,
        scratch_shapes=scratch,
        compiler_params=pltpu.CompilerParams(
            collective_id=0, has_side_effects=True, vmem_limit_bytes=60 * 1024 * 1024
        ),
    )(lengths, query_rows[0], key_rows[0], value_rows[0], out_weight, gate_vector, cotangent[0])
    branch, grad_q, grad_k, grad_v, grad_w, grad_g = pl.pallas_call(
        place,
        out_shape=tuple(jax.ShapeDtypeStruct(out.shape, out.dtype) for out in outs),
        in_specs=[vmem] * 6,
        out_specs=(vmem,) * 6,
    )(*outs)
    return branch[None], grad_q[None], grad_k[None], grad_v[None], grad_w, grad_g


def solution(mesh):
    rows = P("dp", "seq", "tensor")
    placed = (rows, rows, rows, P("dp"), P("seq", "tensor"), P("dp", None), rows)
    return jax.shard_map(
        shards,
        mesh=mesh,
        in_specs=placed,
        out_specs=(rows, rows, rows, rows, P("seq", "tensor"), P("dp", "tensor")),
        check_vma=False,
    )
```

```python
import functools
import math

import jax
import jax.numpy as jnp
from jax import lax
from jax.experimental import pallas as pl
from jax.experimental.pallas import tpu as pltpu
from jax.sharding import PartitionSpec as P

HD = 128
NX = 4
NY = 4
NZ = 4
MASKED = -1e30
MESH = pl.DeviceIdType.MESH
BF = jnp.bfloat16
F32 = jnp.float32


def dot_nn(a, b):
    return lax.dot_general(a, b, (((1,), (0,)), ((), ())), preferred_element_type=F32)


def dot_nt(a, b):
    return lax.dot_general(a, b, (((1,), (1,)), ((), ())), preferred_element_type=F32)


def dot_tn(a, b):
    return lax.dot_general(a, b, (((0,), (0,)), ((), ())), preferred_element_type=F32)


SEMS = {}
SEM_COUNT = 0
for sem_name, sem_size in (
    ("wa1", 3), ("wb1", 3), ("wa2", 3), ("wb2", 3), ("q", 3), ("k", 3), ("v", 3),
    ("gz", 3), ("gc", 1), ("gf", 3), ("o", 9), ("st", 3), ("do", 3), ("pc", 1), ("pz", 3),
    ("ga", 3), ("gb", 1), ("at", 3), ("wx", 3), ("wd", 1), ("dl", 3),
    ("dk", 9), ("dv", 9), ("dq", 9), ("gx", 3), ("gy", 3),
):
    SEMS[sem_name] = SEM_COUNT
    SEM_COUNT += sem_size


def kernel(
    len_ref, q_ref, k_ref, v_ref, w_ref, gate_ref, cot_ref,
    br_ref, gq_ref, gk_ref, gv_ref, gw_ref, gg_ref,
    qbuf, kbuf, vbuf, gfull, wfull, scores, pbuf, top, stat, lse, wrow, wcol,
    osend, orecv, att, dobuf, dacc, psib, psrecv, pown, pzsend, pzrecv,
    gt, attb, dw, wxr, wdsend, wdrecv, dls, delta,
    dks, dkr, dvs, dvr, dqs, dqr, dqacc, gxb, gyb,
    ss, rs,
):
    T = q_ref.shape[0]
    DL = q_ref.shape[1]
    NH = DL // HD
    Q = NX * T
    RA = T // 6
    scale = 1.0 / math.sqrt(HD)
    seq = lax.axis_index("seq")
    ten = lax.axis_index("tensor")
    dp = lax.axis_index("dp")
    x = lax.rem(seq, NX)
    y = lax.div(seq, NX)
    zh = lax.div(ten, 2)
    c = lax.rem(ten, 2)

    def xi(d):
        return lax.rem(x + d, NX)

    def yi(d):
        return lax.rem(y + d, NY)

    def zi(d):
        return lax.rem(zh + d, NZ)

    def X(d):
        return {"seq": y * NX + xi(d)}

    def Y(d):
        return {"seq": yi(d) * NX + x}

    def Z(d):
        return {"tensor": zi(d) * 2 + c}

    sibling = {"tensor": zh * 2 + 1 - c}
    twin = {"dp": 1 - dp}

    def rc(name, i, src, dst, peer):
        j = SEMS[name] + i
        return pltpu.make_async_remote_copy(
            src_ref=src, dst_ref=dst, send_sem=ss.at[j], recv_sem=rs.at[j],
            device_id=peer, device_id_type=MESH,
        )

    sent = []

    def go(*args):
        copy = rc(*args)
        copy.start()
        sent.append(copy)
        return copy

    def lanes(h):
        return pl.ds(pl.multiple_of(h * HD, HD), HD)

    barrier = pltpu.get_barrier_semaphore()
    peers = [X(d) for d in (1, 2, 3)] + [Y(d) for d in (1, 2, 3)] + [Z(d) for d in (1, 2, 3)]
    peers += [sibling, twin]
    for peer in peers:
        pl.semaphore_signal(barrier, inc=1, device_id=peer, device_id_type=MESH)
    gate_local = gate_ref[:, pl.ds(pl.multiple_of(ten * DL, HD), DL)]
    gfull[ten] = (gate_local * cot_ref[...].astype(F32)).astype(BF)
    qbuf[x] = q_ref[...]
    kbuf[y] = k_ref[...]
    vbuf[y] = v_ref[...]
    wfull[y, x] = w_ref[...]
    wrow[...] = jnp.zeros_like(wrow)
    pl.semaphore_wait(barrier, len(peers))

    wa1 = [go("wa1", d - 1, w_ref.at[0:RA], wfull.at[y, x, 0:RA], X(d)) for d in (1, 2, 3)]
    wb1 = [go("wb1", d - 1, w_ref.at[RA:T], wfull.at[y, x, RA:T], Y(d)) for d in (1, 2, 3)]
    q_in = [go("q", d - 1, q_ref, qbuf.at[x], X(d)) for d in (1, 2, 3)]
    k_in = [go("k", d - 1, k_ref, kbuf.at[y], Y(d)) for d in (1, 2, 3)]
    v_in = [go("v", d - 1, v_ref, vbuf.at[y], Y(d)) for d in (1, 2, 3)]
    g_in = [go("gz", d - 1, gfull.at[ten], gfull.at[ten], Z(d)) for d in (1, 2, 3)]
    g_sib = go("gc", 0, gfull.at[ten], gfull.at[ten], sibling)

    for copy in wa1:
        copy.wait_recv()
    wa2 = [go("wa2", d - 1, wfull.at[y, :, 0:RA], wfull.at[y, :, 0:RA], Y(d)) for d in (1, 2, 3)]
    for copy in wb1:
        copy.wait_recv()
    wb2 = [go("wb2", d - 1, wfull.at[:, x, RA:T], wfull.at[:, x, RA:T], X(d)) for d in (1, 2, 3)]

    for copy in q_in:
        copy.wait_recv()
    length = len_ref[0]
    top[...] = jnp.full_like(top, MASKED)

    def score_block(j):
        rows = (j * NX + x) * T + lax.broadcasted_iota(jnp.int32, (T, 1), 0)
        live = rows < length

        def head(h, carry):
            s = dot_nt(kbuf[j, :, lanes(h)], qbuf[:, :, lanes(h)].reshape(Q, HD)) * scale
            s = jnp.where(live, s, MASKED)
            scores[h, j] = s
            top[pl.ds(h, 1), :] = jnp.maximum(
                top[pl.ds(h, 1), :], jnp.max(s, axis=0, keepdims=True)
            )
            return carry

        lax.fori_loop(0, NH, head, 0)

    score_block(y)
    for d in (3, 1, 2):
        k_in[d - 1].wait_recv()
        score_block(yi(NY - d))

    g_fwd = []
    for d in (1, 3, 2):
        g_in[d - 1].wait_recv()
        t = zi(NZ - d) * 2 + c
        g_fwd.append(go("gf", d - 1, gfull.at[t], gfull.at[t], sibling))

    g_tile = [
        go("ga", d - 1, gfull.at[yi(d) * 2 + c], gt.at[c, y], Y(d)) for d in (1, 2, 3)
    ]
    gt[c, y] = gfull[y * 2 + c]

    for copy in v_in:
        copy.wait_recv()

    stat[x] = jnp.zeros((8, Q), F32)

    def forward_head(h, carry):
        row_top = top[pl.ds(h, 1), :]

        def block(j, total):
            p = jnp.exp(scores[h, j] - row_top)
            pbuf[j] = p.astype(BF)
            return total + jnp.sum(p, axis=0, keepdims=True)

        total = lax.fori_loop(0, NY, block, jnp.zeros((1, Q), F32))
        out_t = dot_tn(vbuf[:, :, lanes(h)].reshape(Q, HD), pbuf[...].reshape(Q, Q))
        out_t = out_t / total
        osend[:, :, lanes(h)] = out_t.T.astype(BF).reshape(NX, T, HD)
        stat[x, pl.ds(h, 1), :] = row_top + jnp.log(total)
        for d in (1, 2, 3):
            rc(
                "o", h * 3 + d - 1, osend.at[xi(d), :, lanes(h)],
                orecv.at[x, :, lanes(h)], X(d),
            ).start()
        return carry

    lax.fori_loop(0, NH, forward_head, 0)
    st_in = [go("st", d - 1, stat.at[x], stat.at[x], X(d)) for d in (1, 2, 3)]
    orecv[x] = osend[x]

    for copy in g_tile:
        copy.wait_recv()
    g_share = go("gb", 0, gt.at[c], gt.at[c], sibling)

    for copy in wa2 + wb2 + g_fwd + [g_sib]:
        copy.wait_recv()

    def weight_rows(t):
        return wfull[lax.div(t, 2), pl.ds(lax.rem(t, 2) * 2, 2)].reshape(2 * T, DL)

    dacc[...] = jnp.zeros_like(dacc)

    def grad_step(t, carry):
        dacc[...] += dot_nn(gfull[t], weight_rows(t))
        return carry

    lax.fori_loop(0, 2 * NZ, grad_step, 0)
    dobuf[x] = dacc[...].astype(BF)
    do_in = [go("do", d - 1, dobuf.at[x], dobuf.at[x], X(d)) for d in (1, 2, 3)]

    for copy in st_in:
        copy.wait_recv()
    for h in range(NH):
        parts = [stat[j, h : h + 1, :] for j in range(NX)]
        high = functools.reduce(jnp.maximum, parts)
        row_lse = high + jnp.log(sum(jnp.exp(part - high) for part in parts))
        lse[h : h + 1, :] = row_lse
        for j in range(NX):
            wrow[h * NX + j : h * NX + j + 1, :] = jnp.exp(parts[j] - row_lse)
    wcol[...] = wrow[...].T

    def o_copy(h, d):
        return rc(
            "o", h * 3 + d - 1, osend.at[xi(d), :, lanes(h)], orecv.at[x, :, lanes(h)], X(d)
        )

    def wait_o(h, carry):
        for d in (1, 2, 3):
            o_copy(h, d).wait_recv()
        return carry

    lax.fori_loop(0, NH, wait_o, 0)
    weights = wcol[pl.ds(pl.multiple_of(x * T, 64), T), :]
    for h in range(NH):
        total = jnp.zeros((T, HD), F32)
        for j in range(NX):
            col = h * NX + j
            total += weights[:, col : col + 1] * orecv[j, :, h * HD : (h + 1) * HD].astype(F32)
        att[:, h * HD : (h + 1) * HD] = total.astype(BF)

    attb[y] = att[...]
    at_in = [go("at", d - 1, att, attb.at[y], Y(d)) for d in (1, 2, 3)]

    def proj_sib(z, carry):
        rows = wfull[z, pl.ds((1 - c) * 2, 2)].reshape(2 * T, DL)
        psib[z] = dot_nt(att[...], rows).astype(BF)
        return carry

    lax.fori_loop(0, NZ, proj_sib, 0)
    p_sib = go("pc", 0, psib, psrecv, sibling)

    def proj_own(z, carry):
        rows = wfull[z, pl.ds(c * 2, 2)].reshape(2 * T, DL)
        pown[z] = dot_nt(att[...], rows)
        return carry

    lax.fori_loop(0, NZ, proj_own, 0)
    p_sib.wait_recv()

    def proj_add(z, carry):
        value = pown[z] + psrecv[z].astype(F32)
        pown[z] = value
        pzsend[z] = value.astype(BF)
        return carry

    lax.fori_loop(0, NZ, proj_add, 0)
    pz = [go("pz", d - 1, pzsend.at[zi(d)], pzrecv.at[d - 1], Z(d)) for d in (1, 2, 3)]

    for copy in do_in:
        copy.wait_recv()
    ones = jnp.ones((8, HD), F32)
    dls[x] = jnp.zeros((8, Q), F32)
    for h in range(NH):
        sl = slice(h * HD, (h + 1) * HD)
        prod = dobuf[:, :, sl].astype(F32) * osend[:, :, sl].astype(F32)
        rows = lax.dot_general(
            ones, prod.reshape(Q, HD), (((1,), (1,)), ((), ())),
            preferred_element_type=F32, precision=lax.Precision.HIGHEST,
        )
        dls[x, h : h + 1, :] = rows[0:1, :]
    dl_in = [go("dl", d - 1, dls.at[x], dls.at[x], X(d)) for d in (1, 2, 3)]

    for copy in at_in + [g_share]:
        copy.wait_recv()
    for half in range(2):
        part = dot_tn(gt[half].reshape(NY * T, DL), attb[...].reshape(NY * T, DL))
        dw[2 * half : 2 * half + 2] = part.astype(BF).reshape(2, T, DL)
    wx = [go("wx", d - 1, dw.at[xi(d)], wxr.at[d - 1], X(d)) for d in (1, 2, 3)]

    for copy in dl_in:
        copy.wait_recv()
    for h in range(NH):
        delta[h : h + 1, :] = sum(
            wrow[h * NX + j : h * NX + j + 1, :] * dls[j, h : h + 1, :] for j in range(NX)
        )

    def kv_copy(name, h, d, src, dst):
        return rc(
            name, h * 3 + d - 1, src.at[yi(d), :, lanes(h)], dst.at[d - 1, :, lanes(h)], Y(d)
        )

    def q_copy(h, d):
        return rc("dq", h * 3 + d - 1, dqs.at[xi(d), :, lanes(h)], dqr.at[d - 1, :, lanes(h)], X(d))

    def backward_head(h, carry):
        row_lse = lse[pl.ds(h, 1), :]
        row_delta = delta[pl.ds(h, 1), :]
        dqacc[...] = jnp.zeros_like(dqacc)
        for d in (1, 2, 3, 0):
            j = yi(d)
            grads = dobuf[:, :, lanes(h)].reshape(Q, HD)
            p = jnp.exp(scores[h, j] - row_lse)
            dp_t = dot_nt(vbuf[j, :, lanes(h)], grads)
            ds = (p * (dp_t - row_delta) * scale).astype(BF)
            dvs[j, :, lanes(h)] = dot_nn(p.astype(BF), grads).astype(BF)
            dks[j, :, lanes(h)] = dot_nn(ds, qbuf[:, :, lanes(h)].reshape(Q, HD)).astype(BF)
            if d:
                kv_copy("dv", h, d, dvs, dvr).start()
                kv_copy("dk", h, d, dks, dkr).start()
            dqacc[...] += dot_tn(kbuf[j, :, lanes(h)], ds)
        dqs[:, :, lanes(h)] = dqacc[...].T.astype(BF).reshape(NX, T, HD)
        for d in (1, 2, 3):
            q_copy(h, d).start()
        return carry

    lax.fori_loop(0, NH, backward_head, 0)

    for copy in wx:
        copy.wait_recv()
    total = dw[x].astype(F32)
    for d in (1, 2, 3):
        total += wxr[d - 1].astype(F32)
    wdsend[...] = total.astype(BF)
    wd = go("wd", 0, wdsend, wdrecv, twin)

    for copy in pz:
        copy.wait_recv()
    projected = pown[zh]
    for d in (1, 2, 3):
        projected += pzrecv[d - 1].astype(F32)
    br_ref[...] = (gate_local * projected).astype(BF)
    gxb[x] = jnp.broadcast_to(
        jnp.sum(cot_ref[...].astype(F32) * projected, axis=0, keepdims=True), (8, DL)
    )
    gx = [go("gx", d - 1, gxb.at[x], gxb.at[x], X(d)) for d in (1, 2, 3)]

    for copy in gx:
        copy.wait_recv()
    gyb[y] = gxb[0] + gxb[1] + gxb[2] + gxb[3]
    gy = [go("gy", d - 1, gyb.at[y], gyb.at[y], Y(d)) for d in (1, 2, 3)]

    def wait_grads(h, carry):
        for d in (1, 2, 3):
            kv_copy("dv", h, d, dvs, dvr).wait_recv()
            kv_copy("dk", h, d, dks, dkr).wait_recv()
            q_copy(h, d).wait_recv()
        return carry

    lax.fori_loop(0, NH, wait_grads, 0)
    for out, own, got, index in ((gv_ref, dvs, dvr, y), (gk_ref, dks, dkr, y), (gq_ref, dqs, dqr, x)):
        total = own[index].astype(F32)
        for d in (1, 2, 3):
            total += got[d - 1].astype(F32)
        out[...] = total.astype(BF)

    wd.wait_recv()
    gw_ref[...] = wdsend[...].astype(F32) + wdrecv[...].astype(F32)
    for copy in gy:
        copy.wait_recv()
    gg_ref[...] = (gyb[0] + gyb[1] + gyb[2] + gyb[3])[0:1, :]

    def wait_sends(h, carry):
        for d in (1, 2, 3):
            o_copy(h, d).wait_send()
            kv_copy("dv", h, d, dvs, dvr).wait_send()
            kv_copy("dk", h, d, dks, dkr).wait_send()
            q_copy(h, d).wait_send()
        return carry

    lax.fori_loop(0, NH, wait_sends, 0)
    for copy in sent:
        copy.wait_send()


def place(*refs):
    for i in range(6):
        refs[6 + i][...] = refs[i][...]


def shards(query_rows, key_rows, value_rows, lengths, out_weight, gate_vector, cotangent):
    T, DL = query_rows.shape[1:]
    NH = DL // HD
    Q = NX * T

    def vm(shape, dtype=BF):
        return pltpu.VMEM(shape, dtype)

    blocks = (4, T, DL)
    three = (3, T, DL)
    scratch = [
        vm(blocks), vm(blocks), vm(blocks), vm((2 * NZ, T, DL)), vm((NY, NX, T, DL)),
        vm((NH, NY, T, Q), F32), vm((NY, T, Q)), vm((8, Q), F32), vm((NX, 8, Q), F32),
        vm((8, Q), F32), vm((HD, Q), F32), vm((Q, HD), F32),
        vm(blocks), vm(blocks), vm((T, DL)), vm(blocks), vm((T, DL), F32),
        vm(blocks), vm(blocks), vm(blocks, F32), vm(blocks), vm(three),
        vm((2, NY, T, DL)), vm(blocks), vm(blocks), vm(three),
        vm((T, DL)), vm((T, DL)), vm((NX, 8, Q), F32), vm((8, Q), F32),
        vm(blocks), vm(three), vm(blocks), vm(three), vm(blocks), vm(three), vm((HD, Q), F32),
        vm((NX, 8, DL), F32), vm((NY, 8, DL), F32),
        pltpu.SemaphoreType.DMA((SEM_COUNT,)), pltpu.SemaphoreType.DMA((SEM_COUNT,)),
    ]
    vmem = pl.BlockSpec(memory_space=pltpu.VMEM)
    rows = jax.ShapeDtypeStruct((T, DL), BF)
    outs = pl.pallas_call(
        kernel,
        out_shape=(
            rows, rows, rows, rows,
            jax.ShapeDtypeStruct((T, DL), F32),
            jax.ShapeDtypeStruct((1, DL), F32),
        ),
        in_specs=[pl.BlockSpec(memory_space=pltpu.SMEM)] + [vmem] * 6,
        out_specs=(vmem,) * 6,
        scratch_shapes=scratch,
        compiler_params=pltpu.CompilerParams(
            collective_id=0, has_side_effects=True, vmem_limit_bytes=60 * 1024 * 1024
        ),
    )(lengths, query_rows[0], key_rows[0], value_rows[0], out_weight, gate_vector, cotangent[0])
    branch, grad_q, grad_k, grad_v, grad_w, grad_g = pl.pallas_call(
        place,
        out_shape=tuple(jax.ShapeDtypeStruct(out.shape, out.dtype) for out in outs),
        in_specs=[vmem] * 6,
        out_specs=(vmem,) * 6,
    )(*outs)
    return branch[None], grad_q[None], grad_k[None], grad_v[None], grad_w, grad_g


def solution(mesh):
    rows = P("dp", "seq", "tensor")
    placed = (rows, rows, rows, P("dp"), P("seq", "tensor"), P("dp", None), rows)
    return jax.shard_map(
        shards,
        mesh=mesh,
        in_specs=placed,
        out_specs=(rows, rows, rows, rows, P("seq", "tensor"), P("dp", "tensor")),
        check_vma=False,
    )
```

```python
import functools
import math

import jax
import jax.numpy as jnp
from jax import lax
from jax.experimental import pallas as pl
from jax.experimental.pallas import tpu as pltpu
from jax.sharding import PartitionSpec as P

HD = 128
NX = 4
NY = 4
NZ = 4
MASKED = -1e30
MESH = pl.DeviceIdType.MESH
BF = jnp.bfloat16
F32 = jnp.float32


def dot_nn(a, b):
    return lax.dot_general(a, b, (((1,), (0,)), ((), ())), preferred_element_type=F32)


def dot_nt(a, b):
    return lax.dot_general(a, b, (((1,), (1,)), ((), ())), preferred_element_type=F32)


def dot_tn(a, b):
    return lax.dot_general(a, b, (((0,), (0,)), ((), ())), preferred_element_type=F32)


SEMS = {}
SEM_COUNT = 0
for sem_name, sem_size in (
    ("wa1", 3), ("wb1", 3), ("wa2", 3), ("wb2", 3), ("q", 3), ("k", 3), ("v", 3),
    ("gz", 3), ("gc", 1), ("gf", 3), ("o", 9), ("st", 3), ("do", 3), ("pc", 1), ("pz", 3),
    ("ga", 3), ("gb", 1), ("at", 3), ("wx", 3), ("wd", 1), ("dl", 3),
    ("dk", 9), ("dv", 9), ("dq", 9), ("gx", 3), ("gy", 3),
):
    SEMS[sem_name] = SEM_COUNT
    SEM_COUNT += sem_size


def kernel(
    len_ref, q_ref, k_ref, v_ref, w_ref, gate_ref, cot_ref,
    br_ref, gq_ref, gk_ref, gv_ref, gw_ref, gg_ref,
    qbuf, kbuf, vbuf, gfull, wfull, scores, pbuf, top, stat, lse, wrow, wcol,
    osend, orecv, att, dobuf, dacc, psib, psrecv, pown, pzsend, pzrecv,
    gt, attb, dw, wxr, wdsend, wdrecv, dls, delta,
    dks, dkr, dvs, dvr, dqs, dqr, dqacc, gxb, gyb,
    pad, ss, rs, reach,
):
    T = q_ref.shape[0]
    DL = q_ref.shape[1]
    NH = DL // HD
    Q = NX * T
    RA = T // 3
    scale = 1.0 / math.sqrt(HD)
    seq = lax.axis_index("seq")
    ten = lax.axis_index("tensor")
    dp = lax.axis_index("dp")
    x = lax.rem(seq, NX)
    y = lax.div(seq, NX)
    zh = lax.div(ten, 2)
    c = lax.rem(ten, 2)

    def xi(d):
        return lax.rem(x + d, NX)

    def yi(d):
        return lax.rem(y + d, NY)

    def zi(d):
        return lax.rem(zh + d, NZ)

    def X(d):
        return {"seq": y * NX + xi(d)}

    def Y(d):
        return {"seq": yi(d) * NX + x}

    def Z(d):
        return {"tensor": zi(d) * 2 + c}

    sibling = {"tensor": zh * 2 + 1 - c}
    twin = {"dp": 1 - dp}

    def rc(name, i, src, dst, peer):
        j = SEMS[name] + i
        return pltpu.make_async_remote_copy(
            src_ref=src, dst_ref=dst, send_sem=ss.at[j], recv_sem=rs.at[j],
            device_id=peer, device_id_type=MESH,
        )

    sent = []

    def go(*args):
        copy = rc(*args)
        copy.start()
        sent.append(copy)
        return copy

    def lanes(h):
        return pl.ds(pl.multiple_of(h * HD, HD), HD)

    barrier = pltpu.get_barrier_semaphore()
    near = {"dp": 1 - dp, "tensor": lax.rem(zh + 2 * dp + NZ - 1, NZ) * 2 + c}
    peers = [X(d) for d in (1, 2, 3)] + [Y(d) for d in (1, 2, 3)] + [sibling, twin, near]
    for peer in peers:
        pl.semaphore_signal(barrier, inc=1, device_id=peer, device_id_type=MESH)
    gate_local = gate_ref[:, pl.ds(pl.multiple_of(ten * DL, HD), DL)]
    gfull[ten] = (gate_local * cot_ref[...].astype(F32)).astype(BF)
    qbuf[x] = q_ref[...]
    kbuf[y] = k_ref[...]
    vbuf[y] = v_ref[...]
    wfull[y, x] = w_ref[...]
    wrow[...] = jnp.zeros_like(wrow)
    pad[...] = jnp.zeros_like(pad)
    pl.semaphore_wait(barrier, len(peers))

    wa1 = [go("wa1", d - 1, w_ref.at[0:RA], wfull.at[y, x, 0:RA], X(d)) for d in (1, 2, 3)]
    wb1 = [go("wb1", d - 1, w_ref.at[RA:T], wfull.at[y, x, RA:T], Y(d)) for d in (1, 2, 3)]
    q_in = [go("q", d - 1, q_ref, qbuf.at[x], X(d)) for d in (1, 2, 3)]
    k_in = [go("k", d - 1, k_ref, kbuf.at[y], Y(d)) for d in (1, 2, 3)]
    v_in = [go("v", d - 1, v_ref, vbuf.at[y], Y(d)) for d in (1, 2, 3)]
    for peer in (twin, near):
        pl.semaphore_signal(reach.at[0], inc=1, device_id=peer, device_id_type=MESH)
    pl.semaphore_wait(reach.at[0], 2)
    for peer in (Z(1), Z(3)):
        pl.semaphore_signal(reach.at[1], inc=1, device_id=peer, device_id_type=MESH)
    pl.semaphore_wait(reach.at[1], 2)
    g_in = [go("gz", d - 1, gfull.at[ten], gfull.at[ten], Z(d)) for d in (1, 2, 3)]
    g_sib = go("gc", 0, gfull.at[ten], gfull.at[ten], sibling)

    for copy in wa1:
        copy.wait_recv()
    wa2 = [go("wa2", d - 1, wfull.at[y, :, 0:RA], wfull.at[y, :, 0:RA], Y(d)) for d in (1, 2, 3)]
    for copy in wb1:
        copy.wait_recv()
    wb2 = [go("wb2", d - 1, wfull.at[:, x, RA:T], wfull.at[:, x, RA:T], X(d)) for d in (1, 2, 3)]

    for copy in q_in:
        copy.wait_recv()
    length = len_ref[0]
    top[...] = jnp.full_like(top, MASKED)

    def score_block(j):
        rows = (j * NX + x) * T + lax.broadcasted_iota(jnp.int32, (T, 1), 0)
        live = rows < length

        def head(h, carry):
            s = dot_nt(kbuf[j, :, lanes(h)], qbuf[:, :, lanes(h)].reshape(Q, HD)) * scale
            s = jnp.where(live, s, MASKED)
            scores[h, j] = s
            top[pl.ds(h, 1), :] = jnp.maximum(
                top[pl.ds(h, 1), :], jnp.max(s, axis=0, keepdims=True)
            )
            return carry

        lax.fori_loop(0, NH, head, 0)

    score_block(y)
    for d in (3, 1, 2):
        k_in[d - 1].wait_recv()
        score_block(yi(NY - d))

    g_fwd = []
    for d in (1, 3, 2):
        g_in[d - 1].wait_recv()
        t = zi(NZ - d) * 2 + c
        g_fwd.append(go("gf", d - 1, gfull.at[t], gfull.at[t], sibling))

    for copy in v_in:
        copy.wait_recv()

    stat[x] = jnp.zeros((8, Q), F32)

    def forward_head(h, carry):
        row_top = top[pl.ds(h, 1), :]

        def block(j, total):
            p = jnp.exp(scores[h, j] - row_top)
            pbuf[j] = p.astype(BF)
            return total + jnp.sum(p, axis=0, keepdims=True)

        total = lax.fori_loop(0, NY, block, jnp.zeros((1, Q), F32))
        out_t = dot_tn(vbuf[:, :, lanes(h)].reshape(Q, HD), pbuf[...].reshape(Q, Q))
        out_t = out_t / total
        osend[:, :, lanes(h)] = out_t.T.astype(BF).reshape(NX, T, HD)
        stat[x, pl.ds(h, 1), :] = row_top + jnp.log(total)
        for d in (1, 2, 3):
            rc(
                "o", h * 3 + d - 1, osend.at[xi(d), :, lanes(h)],
                orecv.at[x, :, lanes(h)], X(d),
            ).start()
        return carry

    lax.fori_loop(0, NH, forward_head, 0)
    st_in = [go("st", d - 1, stat.at[x], stat.at[x], X(d)) for d in (1, 2, 3)]
    orecv[x] = osend[x]

    for copy in wa2 + wb2 + g_fwd + [g_sib]:
        copy.wait_recv()

    g_tile = [
        go("ga", d - 1, gfull.at[yi(d) * 2 + c], gt.at[c, y], Y(d)) for d in (1, 2, 3)
    ]
    gt[c, y] = gfull[y * 2 + c]

    def weight_rows(t):
        return wfull[lax.div(t, 2), pl.ds(lax.rem(t, 2) * 2, 2)].reshape(2 * T, DL)

    dacc[...] = jnp.zeros_like(dacc)

    def grad_step(t, carry):
        dacc[...] += dot_nn(gfull[t], weight_rows(t))
        return carry

    lax.fori_loop(0, 2 * NZ, grad_step, 0)
    dobuf[x] = dacc[...].astype(BF)
    do_in = [go("do", d - 1, dobuf.at[x], dobuf.at[x], X(d)) for d in (1, 2, 3)]

    for copy in st_in:
        copy.wait_recv()
    for h in range(NH):
        parts = [stat[j, h : h + 1, :] for j in range(NX)]
        high = functools.reduce(jnp.maximum, parts)
        row_lse = high + jnp.log(sum(jnp.exp(part - high) for part in parts))
        lse[h : h + 1, :] = row_lse
        for j in range(NX):
            wrow[h * NX + j : h * NX + j + 1, :] = jnp.exp(parts[j] - row_lse)
    wcol[...] = wrow[...].T

    def o_copy(h, d):
        return rc(
            "o", h * 3 + d - 1, osend.at[xi(d), :, lanes(h)], orecv.at[x, :, lanes(h)], X(d)
        )

    def wait_o(h, carry):
        for d in (1, 2, 3):
            o_copy(h, d).wait_recv()
        return carry

    lax.fori_loop(0, NH, wait_o, 0)
    weights = wcol[pl.ds(pl.multiple_of(x * T, 64), T), :]
    for h in range(NH):
        total = jnp.zeros((T, HD), F32)
        for j in range(NX):
            col = h * NX + j
            total += weights[:, col : col + 1] * orecv[j, :, h * HD : (h + 1) * HD].astype(F32)
        att[:, h * HD : (h + 1) * HD] = total.astype(BF)

    attb[y] = att[...]
    at_in = [go("at", d - 1, att, attb.at[y], Y(d)) for d in (1, 2, 3)]

    ones = jnp.ones((8, HD), F32)
    dls[x] = jnp.zeros((8, Q), F32)
    own_rows = pl.ds(pl.multiple_of(x * T, 64), T)
    for h in range(NH):
        sl = slice(h * HD, (h + 1) * HD)
        pad[own_rows, :] = dobuf[x, :, sl].astype(F32) * att[:, sl].astype(F32)
        rows = lax.dot_general(
            ones, pad[...], (((1,), (1,)), ((), ())),
            preferred_element_type=F32, precision=lax.Precision.HIGHEST,
        )
        dls[x, h : h + 1, :] = rows[0:1, :]
    dl_in = [go("dl", d - 1, dls.at[x], dls.at[x], X(d)) for d in (1, 2, 3)]

    def proj_sib(z, carry):
        rows = wfull[z, pl.ds((1 - c) * 2, 2)].reshape(2 * T, DL)
        psib[z] = dot_nt(att[...], rows).astype(BF)
        return carry

    lax.fori_loop(0, NZ, proj_sib, 0)
    p_sib = go("pc", 0, psib, psrecv, sibling)

    def proj_own(z, carry):
        rows = wfull[z, pl.ds(c * 2, 2)].reshape(2 * T, DL)
        pown[z] = dot_nt(att[...], rows)
        return carry

    lax.fori_loop(0, NZ, proj_own, 0)
    p_sib.wait_recv()

    def proj_add(z, carry):
        value = pown[z] + psrecv[z].astype(F32)
        pown[z] = value
        pzsend[z] = value.astype(BF)
        return carry

    lax.fori_loop(0, NZ, proj_add, 0)
    pz = [go("pz", d - 1, pzsend.at[zi(d)], pzrecv.at[d - 1], Z(d)) for d in (1, 2, 3)]

    for copy in g_tile:
        copy.wait_recv()
    g_share = go("gb", 0, gt.at[c], gt.at[c], sibling)

    for copy in do_in:
        copy.wait_recv()

    for copy in at_in + [g_share]:
        copy.wait_recv()
    for half in range(2):
        part = dot_tn(gt[half].reshape(NY * T, DL), attb[...].reshape(NY * T, DL))
        dw[2 * half : 2 * half + 2] = part.astype(BF).reshape(2, T, DL)
    wx = [go("wx", d - 1, dw.at[xi(d)], wxr.at[d - 1], X(d)) for d in (1, 2, 3)]

    for copy in dl_in:
        copy.wait_recv()
    for h in range(NH):
        delta[h : h + 1, :] = sum(dls[j, h : h + 1, :] for j in range(NX))

    def kv_copy(name, h, d, src, dst):
        return rc(
            name, h * 3 + d - 1, src.at[yi(d), :, lanes(h)], dst.at[d - 1, :, lanes(h)], Y(d)
        )

    def q_copy(h, d):
        return rc("dq", h * 3 + d - 1, dqs.at[xi(d), :, lanes(h)], dqr.at[d - 1, :, lanes(h)], X(d))

    def backward_head(h, carry):
        row_lse = lse[pl.ds(h, 1), :]
        row_delta = delta[pl.ds(h, 1), :]
        dqacc[...] = jnp.zeros_like(dqacc)
        for d in (1, 2, 3, 0):
            j = yi(d)
            grads = dobuf[:, :, lanes(h)].reshape(Q, HD)
            p = jnp.exp(scores[h, j] - row_lse)
            dp_t = dot_nt(vbuf[j, :, lanes(h)], grads)
            ds = (p * (dp_t - row_delta) * scale).astype(BF)
            dvs[j, :, lanes(h)] = dot_nn(p.astype(BF), grads).astype(BF)
            dks[j, :, lanes(h)] = dot_nn(ds, qbuf[:, :, lanes(h)].reshape(Q, HD)).astype(BF)
            if d:
                kv_copy("dv", h, d, dvs, dvr).start()
                kv_copy("dk", h, d, dks, dkr).start()
            dqacc[...] += dot_tn(kbuf[j, :, lanes(h)], ds)
        dqs[:, :, lanes(h)] = dqacc[...].T.astype(BF).reshape(NX, T, HD)
        for d in (1, 2, 3):
            q_copy(h, d).start()
        return carry

    lax.fori_loop(0, NH, backward_head, 0)

    for copy in wx:
        copy.wait_recv()
    total = dw[x].astype(F32)
    for d in (1, 2, 3):
        total += wxr[d - 1].astype(F32)
    wdsend[...] = total.astype(BF)
    wd = go("wd", 0, wdsend, wdrecv, twin)

    for copy in pz:
        copy.wait_recv()
    projected = pown[zh]
    for d in (1, 2, 3):
        projected += pzrecv[d - 1].astype(F32)
    br_ref[...] = (gate_local * projected).astype(BF)
    gxb[x] = jnp.broadcast_to(
        jnp.sum(cot_ref[...].astype(F32) * projected, axis=0, keepdims=True), (8, DL)
    )
    gx = [go("gx", d - 1, gxb.at[x], gxb.at[x], X(d)) for d in (1, 2, 3)]

    for copy in gx:
        copy.wait_recv()
    gyb[y] = gxb[0] + gxb[1] + gxb[2] + gxb[3]
    gy = [go("gy", d - 1, gyb.at[y], gyb.at[y], Y(d)) for d in (1, 2, 3)]

    def wait_grads(h, carry):
        for d in (1, 2, 3):
            kv_copy("dv", h, d, dvs, dvr).wait_recv()
            kv_copy("dk", h, d, dks, dkr).wait_recv()
            q_copy(h, d).wait_recv()
        return carry

    lax.fori_loop(0, NH, wait_grads, 0)
    for out, own, got, index in ((gv_ref, dvs, dvr, y), (gk_ref, dks, dkr, y), (gq_ref, dqs, dqr, x)):
        total = own[index].astype(F32)
        for d in (1, 2, 3):
            total += got[d - 1].astype(F32)
        out[...] = total.astype(BF)

    wd.wait_recv()
    gw_ref[...] = wdsend[...].astype(F32) + wdrecv[...].astype(F32)
    for copy in gy:
        copy.wait_recv()
    gg_ref[...] = (gyb[0] + gyb[1] + gyb[2] + gyb[3])[0:1, :]

    def wait_sends(h, carry):
        for d in (1, 2, 3):
            o_copy(h, d).wait_send()
            kv_copy("dv", h, d, dvs, dvr).wait_send()
            kv_copy("dk", h, d, dks, dkr).wait_send()
            q_copy(h, d).wait_send()
        return carry

    lax.fori_loop(0, NH, wait_sends, 0)
    for copy in sent:
        copy.wait_send()


def place(*refs):
    for i in range(6):
        refs[6 + i][...] = refs[i][...]


def shards(query_rows, key_rows, value_rows, lengths, out_weight, gate_vector, cotangent):
    T, DL = query_rows.shape[1:]
    NH = DL // HD
    Q = NX * T

    def vm(shape, dtype=BF):
        return pltpu.VMEM(shape, dtype)

    blocks = (4, T, DL)
    three = (3, T, DL)
    scratch = [
        vm(blocks), vm(blocks), vm(blocks), vm((2 * NZ, T, DL)), vm((NY, NX, T, DL)),
        vm((NH, NY, T, Q), F32), vm((NY, T, Q)), vm((8, Q), F32), vm((NX, 8, Q), F32),
        vm((8, Q), F32), vm((HD, Q), F32), vm((Q, HD), F32),
        vm(blocks), vm(blocks), vm((T, DL)), vm(blocks), vm((T, DL), F32),
        vm(blocks), vm(blocks), vm(blocks, F32), vm(blocks), vm(three),
        vm((2, NY, T, DL)), vm(blocks), vm(blocks), vm(three),
        vm((T, DL)), vm((T, DL)), vm((NX, 8, Q), F32), vm((8, Q), F32),
        vm(blocks), vm(three), vm(blocks), vm(three), vm(blocks), vm(three), vm((HD, Q), F32),
        vm((NX, 8, DL), F32), vm((NY, 8, DL), F32),
        vm((Q, HD), F32),
        pltpu.SemaphoreType.DMA((SEM_COUNT,)), pltpu.SemaphoreType.DMA((SEM_COUNT,)),
        pltpu.SemaphoreType.REGULAR((2,)),
    ]
    vmem = pl.BlockSpec(memory_space=pltpu.VMEM)
    rows = jax.ShapeDtypeStruct((T, DL), BF)
    outs = pl.pallas_call(
        kernel,
        out_shape=(
            rows, rows, rows, rows,
            jax.ShapeDtypeStruct((T, DL), F32),
            jax.ShapeDtypeStruct((1, DL), F32),
        ),
        in_specs=[pl.BlockSpec(memory_space=pltpu.SMEM)] + [vmem] * 6,
        out_specs=(vmem,) * 6,
        scratch_shapes=scratch,
        compiler_params=pltpu.CompilerParams(
            collective_id=0, has_side_effects=True, vmem_limit_bytes=60 * 1024 * 1024
        ),
    )(lengths, query_rows[0], key_rows[0], value_rows[0], out_weight, gate_vector, cotangent[0])
    branch, grad_q, grad_k, grad_v, grad_w, grad_g = pl.pallas_call(
        place,
        out_shape=tuple(jax.ShapeDtypeStruct(out.shape, out.dtype) for out in outs),
        in_specs=[vmem] * 6,
        out_specs=(vmem,) * 6,
    )(*outs)
    return branch[None], grad_q[None], grad_k[None], grad_v[None], grad_w, grad_g


def solution(mesh):
    rows = P("dp", "seq", "tensor")
    placed = (rows, rows, rows, P("dp"), P("seq", "tensor"), P("dp", None), rows)
    return jax.shard_map(
        shards,
        mesh=mesh,
        in_specs=placed,
        out_specs=(rows, rows, rows, rows, P("seq", "tensor"), P("dp", "tensor")),
        check_vma=False,
    )
```

```python
import functools
import math

import jax
import jax.numpy as jnp
from jax import lax
from jax.experimental import pallas as pl
from jax.experimental.pallas import tpu as pltpu
from jax.sharding import PartitionSpec as P

HD = 128
NX = 4
NY = 4
NZ = 4
MASKED = -1e30
MESH = pl.DeviceIdType.MESH
BF = jnp.bfloat16
F32 = jnp.float32


def dot_nn(a, b):
    return lax.dot_general(a, b, (((1,), (0,)), ((), ())), preferred_element_type=F32)


def dot_nt(a, b):
    return lax.dot_general(a, b, (((1,), (1,)), ((), ())), preferred_element_type=F32)


def dot_tn(a, b):
    return lax.dot_general(a, b, (((0,), (0,)), ((), ())), preferred_element_type=F32)


SEMS = {}
SEM_COUNT = 0
for sem_name, sem_size in (
    ("wa1", 3), ("wb1", 3), ("wa2", 3), ("wb2", 3), ("q", 3), ("k", 3), ("v", 3),
    ("gz", 3), ("gc", 1), ("gf", 3), ("o", 9), ("st", 3), ("do", 3), ("pc", 1), ("pz", 3),
    ("ga", 3), ("gb", 1), ("at", 3), ("wx", 3), ("wd", 1), ("dl", 3),
    ("dk", 9), ("dv", 9), ("dq", 9), ("gx", 3), ("gy", 3),
):
    SEMS[sem_name] = SEM_COUNT
    SEM_COUNT += sem_size


def kernel(
    len_ref, q_ref, k_ref, v_ref, w_ref, gate_ref, cot_ref,
    br_ref, gq_ref, gk_ref, gv_ref, gw_ref, gg_ref,
    qbuf, kbuf, vbuf, gfull, wfull, scores, pbuf, top, stat, lse, wrow, wcol,
    osend, orecv, att, dobuf, dacc, psib, psrecv, pown, pzsend, pzrecv,
    gt, attb, dw, wxr, wdsend, wdrecv, dls, delta,
    dks, dkr, dvs, dvr, dqs, dqr, dqacc, gxb, gyb,
    pad, ss, rs, reach,
):
    T = q_ref.shape[0]
    DL = q_ref.shape[1]
    NH = DL // HD
    Q = NX * T
    RA = T // 3
    scale = 1.0 / math.sqrt(HD)
    seq = lax.axis_index("seq")
    ten = lax.axis_index("tensor")
    dp = lax.axis_index("dp")
    x = lax.rem(seq, NX)
    y = lax.div(seq, NX)
    zh = lax.div(ten, 2)
    c = lax.rem(ten, 2)

    def xi(d):
        return lax.rem(x + d, NX)

    def yi(d):
        return lax.rem(y + d, NY)

    def zi(d):
        return lax.rem(zh + d, NZ)

    def X(d):
        return {"seq": y * NX + xi(d)}

    def Y(d):
        return {"seq": yi(d) * NX + x}

    def Z(d):
        return {"tensor": zi(d) * 2 + c}

    sibling = {"tensor": zh * 2 + 1 - c}
    twin = {"dp": 1 - dp}

    def rc(name, i, src, dst, peer):
        j = SEMS[name] + i
        return pltpu.make_async_remote_copy(
            src_ref=src, dst_ref=dst, send_sem=ss.at[j], recv_sem=rs.at[j],
            device_id=peer, device_id_type=MESH,
        )

    sent = []

    def go(*args):
        copy = rc(*args)
        copy.start()
        sent.append(copy)
        return copy

    def lanes(h):
        return pl.ds(pl.multiple_of(h * HD, HD), HD)

    barrier = pltpu.get_barrier_semaphore()
    near = {"dp": 1 - dp, "tensor": lax.rem(zh + 2 * dp + NZ - 1, NZ) * 2 + c}
    peers = [X(d) for d in (1, 2, 3)] + [Y(d) for d in (1, 2, 3)] + [sibling, twin, near]
    for peer in peers:
        pl.semaphore_signal(barrier, inc=1, device_id=peer, device_id_type=MESH)
    gate_local = gate_ref[:, pl.ds(pl.multiple_of(ten * DL, HD), DL)]
    gfull[ten] = (gate_local * cot_ref[...].astype(F32)).astype(BF)
    qbuf[x] = q_ref[...]
    kbuf[y] = k_ref[...]
    vbuf[y] = v_ref[...]
    wfull[y, x] = w_ref[...]
    wrow[...] = jnp.zeros_like(wrow)
    pad[...] = jnp.zeros_like(pad)
    pl.semaphore_wait(barrier, len(peers))

    wa1 = [go("wa1", d - 1, w_ref.at[0:RA], wfull.at[y, x, 0:RA], X(d)) for d in (1, 2, 3)]
    wb1 = [go("wb1", d - 1, w_ref.at[RA:T], wfull.at[y, x, RA:T], Y(d)) for d in (1, 2, 3)]
    q_in = [go("q", d - 1, q_ref, qbuf.at[x], X(d)) for d in (1, 2, 3)]
    k_in = [go("k", d - 1, k_ref, kbuf.at[y], Y(d)) for d in (1, 2, 3)]
    v_in = [go("v", d - 1, v_ref, vbuf.at[y], Y(d)) for d in (1, 2, 3)]
    for peer in (twin, near):
        pl.semaphore_signal(reach.at[0], inc=1, device_id=peer, device_id_type=MESH)
    pl.semaphore_wait(reach.at[0], 2)
    for peer in (Z(1), Z(3)):
        pl.semaphore_signal(reach.at[1], inc=1, device_id=peer, device_id_type=MESH)
    pl.semaphore_wait(reach.at[1], 2)
    g_in = [go("gz", d - 1, gfull.at[ten], gfull.at[ten], Z(d)) for d in (1, 2, 3)]
    g_sib = go("gc", 0, gfull.at[ten], gfull.at[ten], sibling)

    for copy in wa1:
        copy.wait_recv()
    wa2 = [go("wa2", d - 1, wfull.at[y, :, 0:RA], wfull.at[y, :, 0:RA], Y(d)) for d in (1, 2, 3)]
    for copy in wb1:
        copy.wait_recv()
    wb2 = [go("wb2", d - 1, wfull.at[:, x, RA:T], wfull.at[:, x, RA:T], X(d)) for d in (1, 2, 3)]

    for copy in q_in:
        copy.wait_recv()
    length = len_ref[0]
    top[...] = jnp.full_like(top, MASKED)

    def score_block(j):
        rows = (j * NX + x) * T + lax.broadcasted_iota(jnp.int32, (T, 1), 0)
        live = rows < length

        def head(h, carry):
            s = dot_nt(kbuf[j, :, lanes(h)], qbuf[:, :, lanes(h)].reshape(Q, HD)) * scale
            s = jnp.where(live, s, MASKED)
            scores[h, j] = s
            top[pl.ds(h, 1), :] = jnp.maximum(
                top[pl.ds(h, 1), :], jnp.max(s, axis=0, keepdims=True)
            )
            return carry

        lax.fori_loop(0, NH, head, 0)

    score_block(y)
    for d in (3, 1, 2):
        k_in[d - 1].wait_recv()
        score_block(yi(NY - d))

    g_fwd = []
    for d in (1, 3, 2):
        g_in[d - 1].wait_recv()
        t = zi(NZ - d) * 2 + c
        g_fwd.append(go("gf", d - 1, gfull.at[t], gfull.at[t], sibling))

    for copy in v_in:
        copy.wait_recv()

    stat[x] = jnp.zeros((8, Q), F32)

    def forward_head(h, carry):
        row_top = top[pl.ds(h, 1), :]

        def block(j, total):
            p = jnp.exp(scores[h, j] - row_top)
            pbuf[j] = p.astype(BF)
            return total + jnp.sum(p, axis=0, keepdims=True)

        total = lax.fori_loop(0, NY, block, jnp.zeros((1, Q), F32))
        out_t = dot_tn(vbuf[:, :, lanes(h)].reshape(Q, HD), pbuf[...].reshape(Q, Q))
        out_t = out_t / total
        osend[:, :, lanes(h)] = out_t.T.astype(BF).reshape(NX, T, HD)
        stat[x, pl.ds(h, 1), :] = row_top + jnp.log(total)
        for d in (1, 2, 3):
            rc(
                "o", h * 3 + d - 1, osend.at[xi(d), :, lanes(h)],
                orecv.at[x, :, lanes(h)], X(d),
            ).start()
        return carry

    lax.fori_loop(0, NH, forward_head, 0)
    st_in = [go("st", d - 1, stat.at[x], stat.at[x], X(d)) for d in (1, 2, 3)]
    orecv[x] = osend[x]

    for copy in wa2 + wb2 + g_fwd + [g_sib]:
        copy.wait_recv()

    g_tile = [
        go("ga", d - 1, gfull.at[yi(d) * 2 + c], gt.at[c, y], Y(d)) for d in (1, 2, 3)
    ]
    gt[c, y] = gfull[y * 2 + c]

    def weight_rows(t):
        return wfull[lax.div(t, 2), pl.ds(lax.rem(t, 2) * 2, 2)].reshape(2 * T, DL)

    dacc[...] = jnp.zeros_like(dacc)

    def grad_step(t, carry):
        dacc[...] += dot_nn(gfull[t], weight_rows(t))
        return carry

    lax.fori_loop(0, 2 * NZ, grad_step, 0)
    dobuf[x] = dacc[...].astype(BF)
    do_in = [go("do", d - 1, dobuf.at[x], dobuf.at[x], X(d)) for d in (1, 2, 3)]

    for copy in st_in:
        copy.wait_recv()
    for h in range(NH):
        parts = [stat[j, h : h + 1, :] for j in range(NX)]
        high = functools.reduce(jnp.maximum, parts)
        row_lse = high + jnp.log(sum(jnp.exp(part - high) for part in parts))
        lse[h : h + 1, :] = row_lse
        for j in range(NX):
            wrow[h * NX + j : h * NX + j + 1, :] = jnp.exp(parts[j] - row_lse)
    wcol[...] = wrow[...].T

    def o_copy(h, d):
        return rc(
            "o", h * 3 + d - 1, osend.at[xi(d), :, lanes(h)], orecv.at[x, :, lanes(h)], X(d)
        )

    def wait_o(h, carry):
        for d in (1, 2, 3):
            o_copy(h, d).wait_recv()
        return carry

    lax.fori_loop(0, NH, wait_o, 0)
    weights = wcol[pl.ds(pl.multiple_of(x * T, 64), T), :]
    for h in range(NH):
        total = jnp.zeros((T, HD), F32)
        for j in range(NX):
            col = h * NX + j
            total += weights[:, col : col + 1] * orecv[j, :, h * HD : (h + 1) * HD].astype(F32)
        att[:, h * HD : (h + 1) * HD] = total.astype(BF)

    attb[y] = att[...]
    at_in = [go("at", d - 1, att, attb.at[y], Y(d)) for d in (1, 2, 3)]

    lane = lax.broadcasted_iota(jnp.int32, (T, HD), 1)
    columns = jnp.zeros((T, HD), F32)
    for h in range(NH):
        sl = slice(h * HD, (h + 1) * HD)
        prod = dobuf[x, :, sl].astype(F32) * att[:, sl].astype(F32)
        columns = jnp.where(lane == h, jnp.sum(prod, axis=1, keepdims=True), columns)
    pad[pl.ds(pl.multiple_of(x * T, 64), T), :] = columns
    dls[x] = pad[...].T[0:8, :]
    dl_in = [go("dl", d - 1, dls.at[x], dls.at[x], X(d)) for d in (1, 2, 3)]

    for copy in g_tile:
        copy.wait_recv()
    g_share = go("gb", 0, gt.at[c], gt.at[c], sibling)

    def proj_sib(z, carry):
        rows = wfull[z, pl.ds((1 - c) * 2, 2)].reshape(2 * T, DL)
        psib[z] = dot_nt(att[...], rows).astype(BF)
        return carry

    lax.fori_loop(0, NZ, proj_sib, 0)
    p_sib = go("pc", 0, psib, psrecv, sibling)

    def proj_own(z, carry):
        rows = wfull[z, pl.ds(c * 2, 2)].reshape(2 * T, DL)
        pown[z] = dot_nt(att[...], rows)
        return carry

    lax.fori_loop(0, NZ, proj_own, 0)
    p_sib.wait_recv()

    def proj_add(z, carry):
        value = pown[z] + psrecv[z].astype(F32)
        pown[z] = value
        pzsend[z] = value.astype(BF)
        return carry

    lax.fori_loop(0, NZ, proj_add, 0)
    pz = [go("pz", d - 1, pzsend.at[zi(d)], pzrecv.at[d - 1], Z(d)) for d in (1, 2, 3)]

    for copy in do_in:
        copy.wait_recv()

    for copy in dl_in:
        copy.wait_recv()
    for h in range(NH):
        delta[h : h + 1, :] = sum(dls[j, h : h + 1, :] for j in range(NX))

    def kv_copy(name, h, d, src, dst):
        return rc(
            name, h * 3 + d - 1, src.at[yi(d), :, lanes(h)], dst.at[d - 1, :, lanes(h)], Y(d)
        )

    def q_copy(h, d):
        return rc("dq", h * 3 + d - 1, dqs.at[xi(d), :, lanes(h)], dqr.at[d - 1, :, lanes(h)], X(d))

    def backward_head(h, carry):
        row_lse = lse[pl.ds(h, 1), :]
        row_delta = delta[pl.ds(h, 1), :]
        dqacc[...] = jnp.zeros_like(dqacc)
        for d in (1, 2, 3, 0):
            j = yi(d)
            grads = dobuf[:, :, lanes(h)].reshape(Q, HD)
            p = jnp.exp(scores[h, j] - row_lse)
            dp_t = dot_nt(vbuf[j, :, lanes(h)], grads)
            ds = (p * (dp_t - row_delta) * scale).astype(BF)
            dvs[j, :, lanes(h)] = dot_nn(p.astype(BF), grads).astype(BF)
            dks[j, :, lanes(h)] = dot_nn(ds, qbuf[:, :, lanes(h)].reshape(Q, HD)).astype(BF)
            if d:
                kv_copy("dv", h, d, dvs, dvr).start()
                kv_copy("dk", h, d, dks, dkr).start()
            dqacc[...] += dot_tn(kbuf[j, :, lanes(h)], ds)
        dqs[:, :, lanes(h)] = dqacc[...].T.astype(BF).reshape(NX, T, HD)
        for d in (1, 2, 3):
            q_copy(h, d).start()
        return carry

    lax.fori_loop(0, 1, backward_head, 0)

    for copy in at_in + [g_share]:
        copy.wait_recv()
    for half in range(2):
        part = dot_tn(gt[half].reshape(NY * T, DL), attb[...].reshape(NY * T, DL))
        dw[2 * half : 2 * half + 2] = part.astype(BF).reshape(2, T, DL)
    wx = [go("wx", d - 1, dw.at[xi(d)], wxr.at[d - 1], X(d)) for d in (1, 2, 3)]

    lax.fori_loop(1, NH, backward_head, 0)

    for copy in wx:
        copy.wait_recv()
    total = dw[x].astype(F32)
    for d in (1, 2, 3):
        total += wxr[d - 1].astype(F32)
    wdsend[...] = total.astype(BF)
    wd = go("wd", 0, wdsend, wdrecv, twin)

    for copy in pz:
        copy.wait_recv()
    projected = pown[zh]
    for d in (1, 2, 3):
        projected += pzrecv[d - 1].astype(F32)
    br_ref[...] = (gate_local * projected).astype(BF)
    gxb[x] = jnp.broadcast_to(
        jnp.sum(cot_ref[...].astype(F32) * projected, axis=0, keepdims=True), (8, DL)
    )
    gx = [go("gx", d - 1, gxb.at[x], gxb.at[x], X(d)) for d in (1, 2, 3)]

    for copy in gx:
        copy.wait_recv()
    gyb[y] = gxb[0] + gxb[1] + gxb[2] + gxb[3]
    gy = [go("gy", d - 1, gyb.at[y], gyb.at[y], Y(d)) for d in (1, 2, 3)]

    def wait_grads(h, carry):
        for d in (1, 2, 3):
            kv_copy("dv", h, d, dvs, dvr).wait_recv()
            kv_copy("dk", h, d, dks, dkr).wait_recv()
            q_copy(h, d).wait_recv()
        return carry

    lax.fori_loop(0, NH, wait_grads, 0)
    for out, own, got, index in ((gv_ref, dvs, dvr, y), (gk_ref, dks, dkr, y), (gq_ref, dqs, dqr, x)):
        total = own[index].astype(F32)
        for d in (1, 2, 3):
            total += got[d - 1].astype(F32)
        out[...] = total.astype(BF)

    wd.wait_recv()
    gw_ref[...] = wdsend[...].astype(F32) + wdrecv[...].astype(F32)
    for copy in gy:
        copy.wait_recv()
    gg_ref[...] = (gyb[0] + gyb[1] + gyb[2] + gyb[3])[0:1, :]

    def wait_sends(h, carry):
        for d in (1, 2, 3):
            o_copy(h, d).wait_send()
            kv_copy("dv", h, d, dvs, dvr).wait_send()
            kv_copy("dk", h, d, dks, dkr).wait_send()
            q_copy(h, d).wait_send()
        return carry

    lax.fori_loop(0, NH, wait_sends, 0)
    for copy in sent:
        copy.wait_send()


def place(*refs):
    for i in range(6):
        refs[6 + i][...] = refs[i][...]


def shards(query_rows, key_rows, value_rows, lengths, out_weight, gate_vector, cotangent):
    T, DL = query_rows.shape[1:]
    NH = DL // HD
    Q = NX * T

    def vm(shape, dtype=BF):
        return pltpu.VMEM(shape, dtype)

    blocks = (4, T, DL)
    three = (3, T, DL)
    scratch = [
        vm(blocks), vm(blocks), vm(blocks), vm((2 * NZ, T, DL)), vm((NY, NX, T, DL)),
        vm((NH, NY, T, Q), F32), vm((NY, T, Q)), vm((8, Q), F32), vm((NX, 8, Q), F32),
        vm((8, Q), F32), vm((HD, Q), F32), vm((Q, HD), F32),
        vm(blocks), vm(blocks), vm((T, DL)), vm(blocks), vm((T, DL), F32),
        vm(blocks), vm(blocks), vm(blocks, F32), vm(blocks), vm(three),
        vm((2, NY, T, DL)), vm(blocks), vm(blocks), vm(three),
        vm((T, DL)), vm((T, DL)), vm((NX, 8, Q), F32), vm((8, Q), F32),
        vm(blocks), vm(three), vm(blocks), vm(three), vm(blocks), vm(three), vm((HD, Q), F32),
        vm((NX, 8, DL), F32), vm((NY, 8, DL), F32),
        vm((Q, HD), F32),
        pltpu.SemaphoreType.DMA((SEM_COUNT,)), pltpu.SemaphoreType.DMA((SEM_COUNT,)),
        pltpu.SemaphoreType.REGULAR((2,)),
    ]
    vmem = pl.BlockSpec(memory_space=pltpu.VMEM)
    rows = jax.ShapeDtypeStruct((T, DL), BF)
    outs = pl.pallas_call(
        kernel,
        out_shape=(
            rows, rows, rows, rows,
            jax.ShapeDtypeStruct((T, DL), F32),
            jax.ShapeDtypeStruct((1, DL), F32),
        ),
        in_specs=[pl.BlockSpec(memory_space=pltpu.SMEM)] + [vmem] * 6,
        out_specs=(vmem,) * 6,
        scratch_shapes=scratch,
        compiler_params=pltpu.CompilerParams(
            collective_id=0, has_side_effects=True, vmem_limit_bytes=60 * 1024 * 1024
        ),
    )(lengths, query_rows[0], key_rows[0], value_rows[0], out_weight, gate_vector, cotangent[0])
    branch, grad_q, grad_k, grad_v, grad_w, grad_g = pl.pallas_call(
        place,
        out_shape=tuple(jax.ShapeDtypeStruct(out.shape, out.dtype) for out in outs),
        in_specs=[vmem] * 6,
        out_specs=(vmem,) * 6,
    )(*outs)
    return branch[None], grad_q[None], grad_k[None], grad_v[None], grad_w, grad_g


def solution(mesh):
    rows = P("dp", "seq", "tensor")
    placed = (rows, rows, rows, P("dp"), P("seq", "tensor"), P("dp", None), rows)
    return jax.shard_map(
        shards,
        mesh=mesh,
        in_specs=placed,
        out_specs=(rows, rows, rows, rows, P("seq", "tensor"), P("dp", "tensor")),
        check_vma=False,
    )
```

```python
import functools
import math

import jax
import jax.numpy as jnp
from jax import lax
from jax.experimental import pallas as pl
from jax.experimental.pallas import tpu as pltpu
from jax.sharding import PartitionSpec as P

HD = 128
NX = 4
NY = 4
NZ = 4
MASKED = -1e30
MESH = pl.DeviceIdType.MESH
BF = jnp.bfloat16
F32 = jnp.float32


def dot_nn(a, b):
    return lax.dot_general(a, b, (((1,), (0,)), ((), ())), preferred_element_type=F32)


def dot_nt(a, b):
    return lax.dot_general(a, b, (((1,), (1,)), ((), ())), preferred_element_type=F32)


def dot_tn(a, b):
    return lax.dot_general(a, b, (((0,), (0,)), ((), ())), preferred_element_type=F32)


SEMS = {}
SEM_COUNT = 0
for sem_name, sem_size in (
    ("wa1", 3), ("wb1", 3), ("wa2", 3), ("wb2", 3), ("q", 3), ("k", 3), ("v", 3),
    ("gz", 3), ("gc", 1), ("gf", 3), ("o", 9), ("st", 3), ("do", 3), ("pc", 4), ("pz", 3),
    ("ga", 3), ("gb", 1), ("at", 3), ("wx", 3), ("wd", 1), ("dl", 3),
    ("dk", 9), ("dv", 9), ("dq", 9), ("gx", 15),
):
    SEMS[sem_name] = SEM_COUNT
    SEM_COUNT += sem_size


def kernel(
    len_ref, q_ref, k_ref, v_ref, w_ref, gate_ref, cot_ref,
    br_ref, gq_ref, gk_ref, gv_ref, gw_ref, gg_ref,
    qbuf, kbuf, vbuf, gfull, wfull, scores, pbuf, top, stat, lse, wrow, wcol,
    osend, orecv, att, dobuf, dacc, psib, psrecv, pown, pzsend, pzrecv,
    gt, attb, dw, wxr, wdsend, wdrecv, dls, delta,
    dks, dkr, dvs, dvr, dqs, dqr, dqacc, gxb,
    pad, ss, rs, reach,
):
    T = q_ref.shape[0]
    DL = q_ref.shape[1]
    NH = DL // HD
    Q = NX * T
    RA = T // 3
    scale = 1.0 / math.sqrt(HD)
    seq = lax.axis_index("seq")
    ten = lax.axis_index("tensor")
    dp = lax.axis_index("dp")
    x = lax.rem(seq, NX)
    y = lax.div(seq, NX)
    zh = lax.div(ten, 2)
    c = lax.rem(ten, 2)

    def xi(d):
        return lax.rem(x + d, NX)

    def yi(d):
        return lax.rem(y + d, NY)

    def zi(d):
        return lax.rem(zh + d, NZ)

    def X(d):
        return {"seq": y * NX + xi(d)}

    def Y(d):
        return {"seq": yi(d) * NX + x}

    def Z(d):
        return {"tensor": zi(d) * 2 + c}

    sibling = {"tensor": zh * 2 + 1 - c}
    twin = {"dp": 1 - dp}

    def rc(name, i, src, dst, peer):
        j = SEMS[name] + i
        return pltpu.make_async_remote_copy(
            src_ref=src, dst_ref=dst, send_sem=ss.at[j], recv_sem=rs.at[j],
            device_id=peer, device_id_type=MESH,
        )

    sent = []

    def go(*args):
        copy = rc(*args)
        copy.start()
        sent.append(copy)
        return copy

    def lanes(h):
        return pl.ds(pl.multiple_of(h * HD, HD), HD)

    barrier = pltpu.get_barrier_semaphore()
    near = {"dp": 1 - dp, "tensor": lax.rem(zh + 2 * dp + NZ - 1, NZ) * 2 + c}
    peers = [X(d) for d in (1, 2, 3)] + [Y(d) for d in (1, 2, 3)] + [sibling, twin, near]
    for peer in peers:
        pl.semaphore_signal(barrier, inc=1, device_id=peer, device_id_type=MESH)
    gate_local = gate_ref[:, pl.ds(pl.multiple_of(ten * DL, HD), DL)]
    gfull[ten] = (gate_local * cot_ref[...].astype(F32)).astype(BF)
    qbuf[x] = q_ref[...]
    kbuf[y] = k_ref[...]
    vbuf[y] = v_ref[...]
    wfull[y, x] = w_ref[...]
    wrow[...] = jnp.zeros_like(wrow)
    pad[...] = jnp.zeros_like(pad)
    pl.semaphore_wait(barrier, len(peers))

    wa1 = [go("wa1", d - 1, w_ref.at[0:RA], wfull.at[y, x, 0:RA], X(d)) for d in (1, 2, 3)]
    wb1 = [go("wb1", d - 1, w_ref.at[RA:T], wfull.at[y, x, RA:T], Y(d)) for d in (1, 2, 3)]
    q_in = [go("q", d - 1, q_ref, qbuf.at[x], X(d)) for d in (1, 2, 3)]
    k_in = [go("k", d - 1, k_ref, kbuf.at[y], Y(d)) for d in (1, 2, 3)]
    v_in = [go("v", d - 1, v_ref, vbuf.at[y], Y(d)) for d in (1, 2, 3)]
    for peer in (twin, near):
        pl.semaphore_signal(reach.at[0], inc=1, device_id=peer, device_id_type=MESH)
    pl.semaphore_wait(reach.at[0], 2)
    for peer in (Z(1), Z(3)):
        pl.semaphore_signal(reach.at[1], inc=1, device_id=peer, device_id_type=MESH)
    pl.semaphore_wait(reach.at[1], 2)
    g_in = [go("gz", d - 1, gfull.at[ten], gfull.at[ten], Z(d)) for d in (1, 2, 3)]
    g_sib = go("gc", 0, gfull.at[ten], gfull.at[ten], sibling)

    for copy in wa1:
        copy.wait_recv()
    wa2 = [go("wa2", d - 1, wfull.at[y, :, 0:RA], wfull.at[y, :, 0:RA], Y(d)) for d in (1, 2, 3)]
    for copy in wb1:
        copy.wait_recv()
    wb2 = [go("wb2", d - 1, wfull.at[:, x, RA:T], wfull.at[:, x, RA:T], X(d)) for d in (1, 2, 3)]

    for copy in q_in:
        copy.wait_recv()
    length = len_ref[0]
    top[...] = jnp.full_like(top, MASKED)

    def score_block(j):
        rows = (j * NX + x) * T + lax.broadcasted_iota(jnp.int32, (T, 1), 0)
        live = rows < length

        def head(h, carry):
            s = dot_nt(kbuf[j, :, lanes(h)], qbuf[:, :, lanes(h)].reshape(Q, HD)) * scale
            s = jnp.where(live, s, MASKED)
            scores[h, j] = s
            top[pl.ds(h, 1), :] = jnp.maximum(
                top[pl.ds(h, 1), :], jnp.max(s, axis=0, keepdims=True)
            )
            return carry

        lax.fori_loop(0, NH, head, 0)

    score_block(y)
    for d in (3, 1, 2):
        k_in[d - 1].wait_recv()
        score_block(yi(NY - d))

    g_fwd = []
    for d in (1, 3, 2):
        g_in[d - 1].wait_recv()
        t = zi(NZ - d) * 2 + c
        g_fwd.append(go("gf", d - 1, gfull.at[t], gfull.at[t], sibling))

    for copy in v_in:
        copy.wait_recv()

    stat[x] = jnp.zeros((8, Q), F32)

    def forward_head(h, carry):
        row_top = top[pl.ds(h, 1), :]

        def block(j, total):
            p = jnp.exp(scores[h, j] - row_top)
            pbuf[j] = p.astype(BF)
            return total + jnp.sum(p, axis=0, keepdims=True)

        total = lax.fori_loop(0, NY, block, jnp.zeros((1, Q), F32))
        out_t = dot_tn(vbuf[:, :, lanes(h)].reshape(Q, HD), pbuf[...].reshape(Q, Q))
        out_t = out_t / total
        osend[:, :, lanes(h)] = out_t.T.astype(BF).reshape(NX, T, HD)
        stat[x, pl.ds(h, 1), :] = row_top + jnp.log(total)
        for d in (1, 2, 3):
            rc(
                "o", h * 3 + d - 1, osend.at[xi(d), :, lanes(h)],
                orecv.at[x, :, lanes(h)], X(d),
            ).start()
        return carry

    lax.fori_loop(0, NH, forward_head, 0)
    st_in = [go("st", d - 1, stat.at[x], stat.at[x], X(d)) for d in (1, 2, 3)]
    orecv[x] = osend[x]

    for copy in wa2 + wb2 + g_fwd + [g_sib]:
        copy.wait_recv()

    g_tile = [
        go("ga", d - 1, gfull.at[yi(d) * 2 + c], gt.at[c, y], Y(d)) for d in (1, 2, 3)
    ]
    gt[c, y] = gfull[y * 2 + c]

    def weight_rows(t):
        return wfull[lax.div(t, 2), pl.ds(lax.rem(t, 2) * 2, 2)].reshape(2 * T, DL)

    dacc[...] = jnp.zeros_like(dacc)

    def grad_step(t, carry):
        dacc[...] += dot_nn(gfull[t], weight_rows(t))
        return carry

    lax.fori_loop(0, 2 * NZ, grad_step, 0)
    dobuf[x] = dacc[...].astype(BF)
    do_in = [go("do", d - 1, dobuf.at[x], dobuf.at[x], X(d)) for d in (1, 2, 3)]

    for copy in st_in:
        copy.wait_recv()
    for h in range(NH):
        parts = [stat[j, h : h + 1, :] for j in range(NX)]
        high = functools.reduce(jnp.maximum, parts)
        row_lse = high + jnp.log(sum(jnp.exp(part - high) for part in parts))
        lse[h : h + 1, :] = row_lse
        for j in range(NX):
            wrow[h * NX + j : h * NX + j + 1, :] = jnp.exp(parts[j] - row_lse)
    wcol[...] = wrow[...].T

    def o_copy(h, d):
        return rc(
            "o", h * 3 + d - 1, osend.at[xi(d), :, lanes(h)], orecv.at[x, :, lanes(h)], X(d)
        )

    def wait_o(h, carry):
        for d in (1, 2, 3):
            o_copy(h, d).wait_recv()
        return carry

    lax.fori_loop(0, NH, wait_o, 0)
    weights = wcol[pl.ds(pl.multiple_of(x * T, 64), T), :]
    for h in range(NH):
        total = jnp.zeros((T, HD), F32)
        for j in range(NX):
            col = h * NX + j
            total += weights[:, col : col + 1] * orecv[j, :, h * HD : (h + 1) * HD].astype(F32)
        att[:, h * HD : (h + 1) * HD] = total.astype(BF)

    p_sib = {}
    for d in (2, 1, 3, 0):
        z = zi(d)
        rows = wfull[z, pl.ds((1 - c) * 2, 2)].reshape(2 * T, DL)
        psib[z] = dot_nt(att[...], rows).astype(BF)
        p_sib[d] = go("pc", d, psib.at[z], psrecv.at[z], sibling)

    attb[y] = att[...]
    at_in = [go("at", d - 1, att, attb.at[y], Y(d)) for d in (1, 2, 3)]

    pz = []
    for d in (2, 1, 3, 0):
        z = zi(d)
        rows = wfull[z, pl.ds(c * 2, 2)].reshape(2 * T, DL)
        value = dot_nt(att[...], rows)
        p_sib[d].wait_recv()
        value += psrecv[z].astype(F32)
        if d:
            pzsend[z] = value.astype(BF)
            pz.append(go("pz", d - 1, pzsend.at[z], pzrecv.at[d - 1], Z(d)))
        else:
            pown[...] = value

    lane = lax.broadcasted_iota(jnp.int32, (T, HD), 1)
    columns = jnp.zeros((T, HD), F32)
    for h in range(NH):
        sl = slice(h * HD, (h + 1) * HD)
        prod = dobuf[x, :, sl].astype(F32) * att[:, sl].astype(F32)
        columns = jnp.where(lane == h, jnp.sum(prod, axis=1, keepdims=True), columns)
    pad[pl.ds(pl.multiple_of(x * T, 64), T), :] = columns
    dls[x] = pad[...].T[0:8, :]
    dl_in = [go("dl", d - 1, dls.at[x], dls.at[x], X(d)) for d in (1, 2, 3)]

    for copy in g_tile:
        copy.wait_recv()
    g_share = go("gb", 0, gt.at[c], gt.at[c], sibling)

    for copy in do_in:
        copy.wait_recv()

    for copy in dl_in:
        copy.wait_recv()
    for h in range(NH):
        delta[h : h + 1, :] = sum(dls[j, h : h + 1, :] for j in range(NX))

    def kv_copy(name, h, d, src, dst):
        return rc(
            name, h * 3 + d - 1, src.at[yi(d), :, lanes(h)], dst.at[d - 1, :, lanes(h)], Y(d)
        )

    def q_copy(h, d):
        return rc("dq", h * 3 + d - 1, dqs.at[xi(d), :, lanes(h)], dqr.at[d - 1, :, lanes(h)], X(d))

    def backward_head(h, carry):
        row_lse = lse[pl.ds(h, 1), :]
        row_delta = delta[pl.ds(h, 1), :]
        dqacc[...] = jnp.zeros_like(dqacc)
        for d in (1, 2, 3, 0):
            j = yi(d)
            grads = dobuf[:, :, lanes(h)].reshape(Q, HD)
            p = jnp.exp(scores[h, j] - row_lse)
            dp_t = dot_nt(vbuf[j, :, lanes(h)], grads)
            ds = (p * (dp_t - row_delta) * scale).astype(BF)
            dvs[j, :, lanes(h)] = dot_nn(p.astype(BF), grads).astype(BF)
            dks[j, :, lanes(h)] = dot_nn(ds, qbuf[:, :, lanes(h)].reshape(Q, HD)).astype(BF)
            if d:
                kv_copy("dv", h, d, dvs, dvr).start()
                kv_copy("dk", h, d, dks, dkr).start()
            dqacc[...] += dot_tn(kbuf[j, :, lanes(h)], ds)
        dqs[:, :, lanes(h)] = dqacc[...].T.astype(BF).reshape(NX, T, HD)
        for d in (1, 2, 3):
            q_copy(h, d).start()
        return carry

    lax.fori_loop(0, 1, backward_head, 0)

    for copy in at_in + [g_share]:
        copy.wait_recv()
    for half in range(2):
        part = dot_tn(gt[half].reshape(NY * T, DL), attb[...].reshape(NY * T, DL))
        dw[2 * half : 2 * half + 2] = part.astype(BF).reshape(2, T, DL)
    wx = [go("wx", d - 1, dw.at[xi(d)], wxr.at[d - 1], X(d)) for d in (1, 2, 3)]

    lax.fori_loop(1, NH, backward_head, 0)

    for copy in wx:
        copy.wait_recv()
    total = dw[x].astype(F32)
    for d in (1, 2, 3):
        total += wxr[d - 1].astype(F32)
    wdsend[...] = total.astype(BF)
    wd = go("wd", 0, wdsend, wdrecv, twin)

    for copy in pz:
        copy.wait_recv()
    projected = pown[...]
    for d in (1, 2, 3):
        projected += pzrecv[d - 1].astype(F32)
    br_ref[...] = (gate_local * projected).astype(BF)
    gxb[seq] = jnp.broadcast_to(
        jnp.sum(cot_ref[...].astype(F32) * projected, axis=0, keepdims=True), (8, DL)
    )
    gx = [
        go("gx", n - 1, gxb.at[seq], gxb.at[seq], {"seq": yi(n // NX) * NX + xi(n % NX)})
        for n in range(1, NX * NY)
    ]

    def wait_grads(h, carry):
        for d in (1, 2, 3):
            kv_copy("dv", h, d, dvs, dvr).wait_recv()
            kv_copy("dk", h, d, dks, dkr).wait_recv()
            q_copy(h, d).wait_recv()
        return carry

    lax.fori_loop(0, NH, wait_grads, 0)
    for out, own, got, index in ((gv_ref, dvs, dvr, y), (gk_ref, dks, dkr, y), (gq_ref, dqs, dqr, x)):
        total = own[index].astype(F32)
        for d in (1, 2, 3):
            total += got[d - 1].astype(F32)
        out[...] = total.astype(BF)

    wd.wait_recv()
    gw_ref[...] = wdsend[...].astype(F32) + wdrecv[...].astype(F32)
    for copy in gx:
        copy.wait_recv()
    gg_ref[...] = sum(gxb[n] for n in range(NX * NY))[0:1, :]

    def wait_sends(h, carry):
        for d in (1, 2, 3):
            o_copy(h, d).wait_send()
            kv_copy("dv", h, d, dvs, dvr).wait_send()
            kv_copy("dk", h, d, dks, dkr).wait_send()
            q_copy(h, d).wait_send()
        return carry

    lax.fori_loop(0, NH, wait_sends, 0)
    for copy in sent:
        copy.wait_send()


def place(*refs):
    for i in range(6):
        refs[6 + i][...] = refs[i][...]


def shards(query_rows, key_rows, value_rows, lengths, out_weight, gate_vector, cotangent):
    T, DL = query_rows.shape[1:]
    NH = DL // HD
    Q = NX * T

    def vm(shape, dtype=BF):
        return pltpu.VMEM(shape, dtype)

    blocks = (4, T, DL)
    three = (3, T, DL)
    scratch = [
        vm(blocks), vm(blocks), vm(blocks), vm((2 * NZ, T, DL)), vm((NY, NX, T, DL)),
        vm((NH, NY, T, Q), F32), vm((NY, T, Q)), vm((8, Q), F32), vm((NX, 8, Q), F32),
        vm((8, Q), F32), vm((HD, Q), F32), vm((Q, HD), F32),
        vm(blocks), vm(blocks), vm((T, DL)), vm(blocks), vm((T, DL), F32),
        vm(blocks), vm(blocks), vm((T, DL), F32), vm(blocks), vm(three),
        vm((2, NY, T, DL)), vm(blocks), vm(blocks), vm(three),
        vm((T, DL)), vm((T, DL)), vm((NX, 8, Q), F32), vm((8, Q), F32),
        vm(blocks), vm(three), vm(blocks), vm(three), vm(blocks), vm(three), vm((HD, Q), F32),
        vm((NX * NY, 8, DL), F32),
        vm((Q, HD), F32),
        pltpu.SemaphoreType.DMA((SEM_COUNT,)), pltpu.SemaphoreType.DMA((SEM_COUNT,)),
        pltpu.SemaphoreType.REGULAR((2,)),
    ]
    vmem = pl.BlockSpec(memory_space=pltpu.VMEM)
    rows = jax.ShapeDtypeStruct((T, DL), BF)
    outs = pl.pallas_call(
        kernel,
        out_shape=(
            rows, rows, rows, rows,
            jax.ShapeDtypeStruct((T, DL), F32),
            jax.ShapeDtypeStruct((1, DL), F32),
        ),
        in_specs=[pl.BlockSpec(memory_space=pltpu.SMEM)] + [vmem] * 6,
        out_specs=(vmem,) * 6,
        scratch_shapes=scratch,
        compiler_params=pltpu.CompilerParams(
            collective_id=0, has_side_effects=True, vmem_limit_bytes=60 * 1024 * 1024
        ),
    )(lengths, query_rows[0], key_rows[0], value_rows[0], out_weight, gate_vector, cotangent[0])
    branch, grad_q, grad_k, grad_v, grad_w, grad_g = pl.pallas_call(
        place,
        out_shape=tuple(jax.ShapeDtypeStruct(out.shape, out.dtype) for out in outs),
        in_specs=[vmem] * 6,
        out_specs=(vmem,) * 6,
    )(*outs)
    return branch[None], grad_q[None], grad_k[None], grad_v[None], grad_w, grad_g


def solution(mesh):
    rows = P("dp", "seq", "tensor")
    placed = (rows, rows, rows, P("dp"), P("seq", "tensor"), P("dp", None), rows)
    return jax.shard_map(
        shards,
        mesh=mesh,
        in_specs=placed,
        out_specs=(rows, rows, rows, rows, P("seq", "tensor"), P("dp", "tensor")),
        check_vma=False,
    )
```

```python
import functools
import math

import jax
import jax.numpy as jnp
from jax import lax
from jax.experimental import pallas as pl
from jax.experimental.pallas import tpu as pltpu
from jax.sharding import PartitionSpec as P

HD = 128
NX = 4
NY = 4
NZ = 4
MASKED = -1e30
MESH = pl.DeviceIdType.MESH
BF = jnp.bfloat16
F32 = jnp.float32


def dot_nn(a, b):
    return lax.dot_general(a, b, (((1,), (0,)), ((), ())), preferred_element_type=F32)


def dot_nt(a, b):
    return lax.dot_general(a, b, (((1,), (1,)), ((), ())), preferred_element_type=F32)


def dot_tn(a, b):
    return lax.dot_general(a, b, (((0,), (0,)), ((), ())), preferred_element_type=F32)


SEMS = {}
SEM_COUNT = 0
for sem_name, sem_size in (
    ("wa1", 3), ("wb1", 3), ("wa2", 3), ("wb2", 3), ("q", 3), ("k", 3), ("v", 3),
    ("gz", 3), ("gc", 1), ("gf", 3), ("o", 9), ("st", 3), ("do", 3), ("pc", 4), ("pz", 3),
    ("ga", 3), ("gb", 1), ("at", 3), ("wx", 3), ("wd", 1), ("dl", 3),
    ("dk", 9), ("dv", 9), ("dq", 9), ("gx", 15),
):
    SEMS[sem_name] = SEM_COUNT
    SEM_COUNT += sem_size


def kernel(
    len_ref, q_ref, k_ref, v_ref, w_ref, gate_ref, cot_ref,
    br_ref, gq_ref, gk_ref, gv_ref, gw_ref, gg_ref,
    qbuf, kbuf, vbuf, gfull, wfull, scores, pbuf, top, stat, lse, wrow, wcol,
    osend, orecv, att, dobuf, dacc, psib, psrecv, pown, pzsend, pzrecv,
    gt, attb, dw, wxr, wdsend, wdrecv, dls, delta,
    dks, dkr, dvs, dvr, dqs, dqr, dqacc, gxb,
    pad, ss, rs, reach,
):
    T = q_ref.shape[0]
    DL = q_ref.shape[1]
    NH = DL // HD
    Q = NX * T
    RA = T // 2
    scale = 1.0 / math.sqrt(HD)
    seq = lax.axis_index("seq")
    ten = lax.axis_index("tensor")
    dp = lax.axis_index("dp")
    x = lax.rem(seq, NX)
    y = lax.div(seq, NX)
    zh = lax.div(ten, 2)
    c = lax.rem(ten, 2)

    def xi(d):
        return lax.rem(x + d, NX)

    def yi(d):
        return lax.rem(y + d, NY)

    def zi(d):
        return lax.rem(zh + d, NZ)

    def X(d):
        return {"seq": y * NX + xi(d)}

    def Y(d):
        return {"seq": yi(d) * NX + x}

    def Z(d):
        return {"tensor": zi(d) * 2 + c}

    sibling = {"tensor": zh * 2 + 1 - c}
    twin = {"dp": 1 - dp}

    def rc(name, i, src, dst, peer):
        j = SEMS[name] + i
        return pltpu.make_async_remote_copy(
            src_ref=src, dst_ref=dst, send_sem=ss.at[j], recv_sem=rs.at[j],
            device_id=peer, device_id_type=MESH,
        )

    sent = []

    def go(*args):
        copy = rc(*args)
        copy.start()
        sent.append(copy)
        return copy

    def lanes(h):
        return pl.ds(pl.multiple_of(h * HD, HD), HD)

    barrier = pltpu.get_barrier_semaphore()
    near = {"dp": 1 - dp, "tensor": lax.rem(zh + 2 * dp + NZ - 1, NZ) * 2 + c}
    peers = [X(d) for d in (1, 2, 3)] + [Y(d) for d in (1, 2, 3)] + [sibling, twin, near]
    for peer in peers:
        pl.semaphore_signal(barrier, inc=1, device_id=peer, device_id_type=MESH)
    gate_local = gate_ref[:, pl.ds(pl.multiple_of(ten * DL, HD), DL)]
    gfull[ten] = (gate_local * cot_ref[...].astype(F32)).astype(BF)
    qbuf[x] = q_ref[...]
    kbuf[y] = k_ref[...]
    vbuf[y] = v_ref[...]
    wfull[y, x] = w_ref[...]
    wrow[...] = jnp.zeros_like(wrow)
    pad[...] = jnp.zeros_like(pad)
    pl.semaphore_wait(barrier, len(peers))

    wa1 = [go("wa1", d - 1, w_ref.at[0:RA], wfull.at[y, x, 0:RA], X(d)) for d in (1, 2, 3)]
    wb1 = [go("wb1", d - 1, w_ref.at[RA:T], wfull.at[y, x, RA:T], Y(d)) for d in (1, 2, 3)]
    q_in = [go("q", d - 1, q_ref, qbuf.at[x], X(d)) for d in (1, 2, 3)]
    k_in = [go("k", d - 1, k_ref, kbuf.at[y], Y(d)) for d in (1, 2, 3)]
    v_in = [go("v", d - 1, v_ref, vbuf.at[y], Y(d)) for d in (1, 2, 3)]
    for peer in (twin, near):
        pl.semaphore_signal(reach.at[0], inc=1, device_id=peer, device_id_type=MESH)
    pl.semaphore_wait(reach.at[0], 2)
    for peer in (Z(1), Z(3)):
        pl.semaphore_signal(reach.at[1], inc=1, device_id=peer, device_id_type=MESH)
    pl.semaphore_wait(reach.at[1], 2)
    g_in = [go("gz", d - 1, gfull.at[ten], gfull.at[ten], Z(d)) for d in (1, 2, 3)]
    g_sib = go("gc", 0, gfull.at[ten], gfull.at[ten], sibling)

    for copy in wa1:
        copy.wait_recv()
    wa2 = [go("wa2", d - 1, wfull.at[y, :, 0:RA], wfull.at[y, :, 0:RA], Y(d)) for d in (1, 2, 3)]
    for copy in wb1:
        copy.wait_recv()
    wb2 = [go("wb2", d - 1, wfull.at[:, x, RA:T], wfull.at[:, x, RA:T], X(d)) for d in (1, 2, 3)]

    for copy in q_in:
        copy.wait_recv()
    length = len_ref[0]
    top[...] = jnp.full_like(top, MASKED)

    def score_block(j):
        rows = (j * NX + x) * T + lax.broadcasted_iota(jnp.int32, (T, 1), 0)
        live = rows < length

        def head(h, carry):
            s = dot_nt(kbuf[j, :, lanes(h)], qbuf[:, :, lanes(h)].reshape(Q, HD)) * scale
            s = jnp.where(live, s, MASKED)
            scores[h, j] = s
            top[pl.ds(h, 1), :] = jnp.maximum(
                top[pl.ds(h, 1), :], jnp.max(s, axis=0, keepdims=True)
            )
            return carry

        lax.fori_loop(0, NH, head, 0)

    score_block(y)
    for d in (3, 1, 2):
        k_in[d - 1].wait_recv()
        score_block(yi(NY - d))

    g_fwd = []
    for d in (1, 3, 2):
        g_in[d - 1].wait_recv()
        t = zi(NZ - d) * 2 + c
        g_fwd.append(go("gf", d - 1, gfull.at[t], gfull.at[t], sibling))

    for copy in v_in:
        copy.wait_recv()

    stat[x] = jnp.zeros((8, Q), F32)

    def forward_head(h, carry):
        row_top = top[pl.ds(h, 1), :]

        def block(j, total):
            p = jnp.exp(scores[h, j] - row_top)
            pbuf[j] = p.astype(BF)
            return total + jnp.sum(p, axis=0, keepdims=True)

        total = lax.fori_loop(0, NY, block, jnp.zeros((1, Q), F32))
        out_t = dot_tn(vbuf[:, :, lanes(h)].reshape(Q, HD), pbuf[...].reshape(Q, Q))
        out_t = out_t / total
        osend[:, :, lanes(h)] = out_t.T.astype(BF).reshape(NX, T, HD)
        stat[x, pl.ds(h, 1), :] = row_top + jnp.log(total)
        for d in (1, 2, 3):
            rc(
                "o", h * 3 + d - 1, osend.at[xi(d), :, lanes(h)],
                orecv.at[x, :, lanes(h)], X(d),
            ).start()
        return carry

    lax.fori_loop(0, NH, forward_head, 0)
    st_in = [go("st", d - 1, stat.at[x], stat.at[x], X(d)) for d in (1, 2, 3)]
    orecv[x] = osend[x]

    for copy in wa2 + wb2 + g_fwd + [g_sib]:
        copy.wait_recv()

    g_tile = [
        go("ga", d - 1, gfull.at[yi(d) * 2 + c], gt.at[c, y], Y(d)) for d in (1, 2, 3)
    ]
    gt[c, y] = gfull[y * 2 + c]

    def weight_rows(t):
        return wfull[lax.div(t, 2), pl.ds(lax.rem(t, 2) * 2, 2)].reshape(2 * T, DL)

    dacc[...] = jnp.zeros_like(dacc)

    def grad_step(t, carry):
        dacc[...] += dot_nn(gfull[t], weight_rows(t))
        return carry

    lax.fori_loop(0, 2 * NZ, grad_step, 0)
    dobuf[x] = dacc[...].astype(BF)
    do_in = [go("do", d - 1, dobuf.at[x], dobuf.at[x], X(d)) for d in (1, 2, 3)]

    for copy in st_in:
        copy.wait_recv()
    for h in range(NH):
        parts = [stat[j, h : h + 1, :] for j in range(NX)]
        high = functools.reduce(jnp.maximum, parts)
        row_lse = high + jnp.log(sum(jnp.exp(part - high) for part in parts))
        lse[h : h + 1, :] = row_lse
        for j in range(NX):
            wrow[h * NX + j : h * NX + j + 1, :] = jnp.exp(parts[j] - row_lse)
    wcol[...] = wrow[...].T

    def o_copy(h, d):
        return rc(
            "o", h * 3 + d - 1, osend.at[xi(d), :, lanes(h)], orecv.at[x, :, lanes(h)], X(d)
        )

    def wait_o(h, carry):
        for d in (1, 2, 3):
            o_copy(h, d).wait_recv()
        return carry

    lax.fori_loop(0, NH, wait_o, 0)
    weights = wcol[pl.ds(pl.multiple_of(x * T, 64), T), :]
    for h in range(NH):
        total = jnp.zeros((T, HD), F32)
        for j in range(NX):
            col = h * NX + j
            total += weights[:, col : col + 1] * orecv[j, :, h * HD : (h + 1) * HD].astype(F32)
        att[:, h * HD : (h + 1) * HD] = total.astype(BF)

    p_sib = {}
    for d in (2, 1, 3, 0):
        z = zi(d)
        rows = wfull[z, pl.ds((1 - c) * 2, 2)].reshape(2 * T, DL)
        psib[z] = dot_nt(att[...], rows).astype(BF)
        p_sib[d] = go("pc", d, psib.at[z], psrecv.at[z], sibling)

    attb[y] = att[...]
    at_in = [go("at", d - 1, att, attb.at[y], Y(d)) for d in (1, 2, 3)]

    pz = []
    for d in (2, 1, 3, 0):
        z = zi(d)
        rows = wfull[z, pl.ds(c * 2, 2)].reshape(2 * T, DL)
        value = dot_nt(att[...], rows)
        p_sib[d].wait_recv()
        value += psrecv[z].astype(F32)
        if d:
            pzsend[z] = value.astype(BF)
            pz.append(go("pz", d - 1, pzsend.at[z], pzrecv.at[d - 1], Z(d)))
        else:
            pown[...] = value

    lane = lax.broadcasted_iota(jnp.int32, (T, HD), 1)
    columns = jnp.zeros((T, HD), F32)
    for h in range(NH):
        sl = slice(h * HD, (h + 1) * HD)
        prod = dobuf[x, :, sl].astype(F32) * att[:, sl].astype(F32)
        columns = jnp.where(lane == h, jnp.sum(prod, axis=1, keepdims=True), columns)
    pad[pl.ds(pl.multiple_of(x * T, 64), T), :] = columns
    dls[x] = pad[...].T[0:8, :]
    dl_in = [go("dl", d - 1, dls.at[x], dls.at[x], X(d)) for d in (1, 2, 3)]

    for copy in g_tile:
        copy.wait_recv()
    g_share = go("gb", 0, gt.at[c], gt.at[c], sibling)

    for copy in do_in:
        copy.wait_recv()

    for copy in dl_in:
        copy.wait_recv()
    for h in range(NH):
        delta[h : h + 1, :] = sum(dls[j, h : h + 1, :] for j in range(NX))

    def kv_copy(name, h, d, src, dst):
        return rc(
            name, h * 3 + d - 1, src.at[yi(d), :, lanes(h)], dst.at[d - 1, :, lanes(h)], Y(d)
        )

    def q_copy(h, d):
        return rc("dq", h * 3 + d - 1, dqs.at[xi(d), :, lanes(h)], dqr.at[d - 1, :, lanes(h)], X(d))

    def backward_head(h, carry):
        row_lse = lse[pl.ds(h, 1), :]
        row_delta = delta[pl.ds(h, 1), :]
        dqacc[...] = jnp.zeros_like(dqacc)
        for d in (1, 2, 3, 0):
            j = yi(d)
            grads = dobuf[:, :, lanes(h)].reshape(Q, HD)
            p = jnp.exp(scores[h, j] - row_lse)
            dp_t = dot_nt(vbuf[j, :, lanes(h)], grads)
            ds = (p * (dp_t - row_delta) * scale).astype(BF)
            dvs[j, :, lanes(h)] = dot_nn(p.astype(BF), grads).astype(BF)
            dks[j, :, lanes(h)] = dot_nn(ds, qbuf[:, :, lanes(h)].reshape(Q, HD)).astype(BF)
            if d:
                kv_copy("dv", h, d, dvs, dvr).start()
                kv_copy("dk", h, d, dks, dkr).start()
            dqacc[...] += dot_tn(kbuf[j, :, lanes(h)], ds)
        dqs[:, :, lanes(h)] = dqacc[...].T.astype(BF).reshape(NX, T, HD)
        for d in (1, 2, 3):
            q_copy(h, d).start()
        return carry

    lax.fori_loop(0, 1, backward_head, 0)

    for copy in at_in + [g_share]:
        copy.wait_recv()
    for half in range(2):
        part = dot_tn(gt[half].reshape(NY * T, DL), attb[...].reshape(NY * T, DL))
        dw[2 * half : 2 * half + 2] = part.astype(BF).reshape(2, T, DL)
    wx = [go("wx", d - 1, dw.at[xi(d)], wxr.at[d - 1], X(d)) for d in (1, 2, 3)]

    lax.fori_loop(1, NH, backward_head, 0)

    for copy in pz:
        copy.wait_recv()
    projected = pown[...]
    for d in (1, 2, 3):
        projected += pzrecv[d - 1].astype(F32)
    br_ref[...] = (gate_local * projected).astype(BF)
    gxb[seq] = jnp.broadcast_to(
        jnp.sum(cot_ref[...].astype(F32) * projected, axis=0, keepdims=True), (8, DL)
    )
    gx = [
        go("gx", n - 1, gxb.at[seq], gxb.at[seq], {"seq": yi(n // NX) * NX + xi(n % NX)})
        for n in range(1, NX * NY)
    ]

    for copy in wx:
        copy.wait_recv()
    total = dw[x].astype(F32)
    for d in (1, 2, 3):
        total += wxr[d - 1].astype(F32)
    wdsend[...] = total.astype(BF)
    wd = go("wd", 0, wdsend, wdrecv, twin)

    def wait_grads(h, carry):
        for d in (1, 2, 3):
            kv_copy("dv", h, d, dvs, dvr).wait_recv()
            kv_copy("dk", h, d, dks, dkr).wait_recv()
            q_copy(h, d).wait_recv()
        return carry

    lax.fori_loop(0, NH, wait_grads, 0)
    for out, own, got, index in ((gv_ref, dvs, dvr, y), (gk_ref, dks, dkr, y), (gq_ref, dqs, dqr, x)):
        total = own[index].astype(F32)
        for d in (1, 2, 3):
            total += got[d - 1].astype(F32)
        out[...] = total.astype(BF)

    wd.wait_recv()
    gw_ref[...] = wdsend[...].astype(F32) + wdrecv[...].astype(F32)
    for copy in gx:
        copy.wait_recv()
    gg_ref[...] = sum(gxb[n] for n in range(NX * NY))[0:1, :]

    def wait_sends(h, carry):
        for d in (1, 2, 3):
            o_copy(h, d).wait_send()
            kv_copy("dv", h, d, dvs, dvr).wait_send()
            kv_copy("dk", h, d, dks, dkr).wait_send()
            q_copy(h, d).wait_send()
        return carry

    lax.fori_loop(0, NH, wait_sends, 0)
    for copy in sent:
        copy.wait_send()


def place(*refs):
    for i in range(6):
        refs[6 + i][...] = refs[i][...]


def shards(query_rows, key_rows, value_rows, lengths, out_weight, gate_vector, cotangent):
    T, DL = query_rows.shape[1:]
    NH = DL // HD
    Q = NX * T

    def vm(shape, dtype=BF):
        return pltpu.VMEM(shape, dtype)

    blocks = (4, T, DL)
    three = (3, T, DL)
    scratch = [
        vm(blocks), vm(blocks), vm(blocks), vm((2 * NZ, T, DL)), vm((NY, NX, T, DL)),
        vm((NH, NY, T, Q), F32), vm((NY, T, Q)), vm((8, Q), F32), vm((NX, 8, Q), F32),
        vm((8, Q), F32), vm((HD, Q), F32), vm((Q, HD), F32),
        vm(blocks), vm(blocks), vm((T, DL)), vm(blocks), vm((T, DL), F32),
        vm(blocks), vm(blocks), vm((T, DL), F32), vm(blocks), vm(three),
        vm((2, NY, T, DL)), vm(blocks), vm(blocks), vm(three),
        vm((T, DL)), vm((T, DL)), vm((NX, 8, Q), F32), vm((8, Q), F32),
        vm(blocks), vm(three), vm(blocks), vm(three), vm(blocks), vm(three), vm((HD, Q), F32),
        vm((NX * NY, 8, DL), F32),
        vm((Q, HD), F32),
        pltpu.SemaphoreType.DMA((SEM_COUNT,)), pltpu.SemaphoreType.DMA((SEM_COUNT,)),
        pltpu.SemaphoreType.REGULAR((2,)),
    ]
    vmem = pl.BlockSpec(memory_space=pltpu.VMEM)
    rows = jax.ShapeDtypeStruct((T, DL), BF)
    outs = pl.pallas_call(
        kernel,
        out_shape=(
            rows, rows, rows, rows,
            jax.ShapeDtypeStruct((T, DL), F32),
            jax.ShapeDtypeStruct((1, DL), F32),
        ),
        in_specs=[pl.BlockSpec(memory_space=pltpu.SMEM)] + [vmem] * 6,
        out_specs=(vmem,) * 6,
        scratch_shapes=scratch,
        compiler_params=pltpu.CompilerParams(
            collective_id=0, has_side_effects=True, vmem_limit_bytes=60 * 1024 * 1024
        ),
    )(lengths, query_rows[0], key_rows[0], value_rows[0], out_weight, gate_vector, cotangent[0])
    branch, grad_q, grad_k, grad_v, grad_w, grad_g = pl.pallas_call(
        place,
        out_shape=tuple(jax.ShapeDtypeStruct(out.shape, out.dtype) for out in outs),
        in_specs=[vmem] * 6,
        out_specs=(vmem,) * 6,
    )(*outs)
    return branch[None], grad_q[None], grad_k[None], grad_v[None], grad_w, grad_g


def solution(mesh):
    rows = P("dp", "seq", "tensor")
    placed = (rows, rows, rows, P("dp"), P("seq", "tensor"), P("dp", None), rows)
    return jax.shard_map(
        shards,
        mesh=mesh,
        in_specs=placed,
        out_specs=(rows, rows, rows, rows, P("seq", "tensor"), P("dp", "tensor")),
        check_vma=False,
    )
```

```python
import functools
import math

import jax
import jax.numpy as jnp
from jax import lax
from jax.experimental import pallas as pl
from jax.experimental.pallas import tpu as pltpu
from jax.sharding import PartitionSpec as P

HD = 128
NX = 4
NY = 4
NZ = 4
MASKED = -1e30
MESH = pl.DeviceIdType.MESH
BF = jnp.bfloat16
F32 = jnp.float32


def dot_nn(a, b):
    return lax.dot_general(a, b, (((1,), (0,)), ((), ())), preferred_element_type=F32)


def dot_nt(a, b):
    return lax.dot_general(a, b, (((1,), (1,)), ((), ())), preferred_element_type=F32)


def dot_tn(a, b):
    return lax.dot_general(a, b, (((0,), (0,)), ((), ())), preferred_element_type=F32)


SEMS = {}
SEM_COUNT = 0
for sem_name, sem_size in (
    ("wa1", 3), ("wb1", 3), ("wa2", 3), ("wb2", 3), ("q", 3), ("k", 3), ("v", 3),
    ("gz", 3), ("gc", 1), ("gf", 3), ("o", 9), ("st", 3), ("do", 3), ("pc", 4), ("pz", 3),
    ("ga", 3), ("gb", 1), ("at", 3), ("wx", 3), ("wd", 1), ("dl", 3),
    ("dk", 9), ("dv", 9), ("dq", 9), ("gx", 15),
):
    SEMS[sem_name] = SEM_COUNT
    SEM_COUNT += sem_size


def kernel(
    len_ref, q_ref, k_ref, v_ref, w_ref, gate_ref, cot_ref,
    br_ref, gq_ref, gk_ref, gv_ref, gw_ref, gg_ref,
    qbuf, kbuf, vbuf, gfull, wfull, scores, pbuf, top, stat, lse, wrow, wcol,
    osend, orecv, att, dobuf, dacc, psib, psrecv, pown, pzsend, pzrecv,
    gt, attb, dw, wxr, wdsend, wdrecv, dls, delta,
    dks, dkr, dvs, dvr, dqs, dqr, dqacc, gxb,
    pad, ss, rs, reach,
):
    T = q_ref.shape[0]
    DL = q_ref.shape[1]
    NH = DL // HD
    Q = NX * T
    RA = T * 5 // 12
    scale = 1.0 / math.sqrt(HD)
    seq = lax.axis_index("seq")
    ten = lax.axis_index("tensor")
    dp = lax.axis_index("dp")
    x = lax.rem(seq, NX)
    y = lax.div(seq, NX)
    zh = lax.div(ten, 2)
    c = lax.rem(ten, 2)

    def xi(d):
        return lax.rem(x + d, NX)

    def yi(d):
        return lax.rem(y + d, NY)

    def zi(d):
        return lax.rem(zh + d, NZ)

    def X(d):
        return {"seq": y * NX + xi(d)}

    def Y(d):
        return {"seq": yi(d) * NX + x}

    def Z(d):
        return {"tensor": zi(d) * 2 + c}

    sibling = {"tensor": zh * 2 + 1 - c}
    twin = {"dp": 1 - dp}

    def rc(name, i, src, dst, peer):
        j = SEMS[name] + i
        return pltpu.make_async_remote_copy(
            src_ref=src, dst_ref=dst, send_sem=ss.at[j], recv_sem=rs.at[j],
            device_id=peer, device_id_type=MESH,
        )

    sent = []

    def go(*args):
        copy = rc(*args)
        copy.start()
        sent.append(copy)
        return copy

    def lanes(h):
        return pl.ds(pl.multiple_of(h * HD, HD), HD)

    barrier = pltpu.get_barrier_semaphore()
    near = {"dp": 1 - dp, "tensor": lax.rem(zh + 2 * dp + NZ - 1, NZ) * 2 + c}
    peers = [X(d) for d in (1, 2, 3)] + [Y(d) for d in (1, 2, 3)] + [sibling, twin, near]
    for peer in peers:
        pl.semaphore_signal(barrier, inc=1, device_id=peer, device_id_type=MESH)
    gate_local = gate_ref[:, pl.ds(pl.multiple_of(ten * DL, HD), DL)]
    gfull[ten] = (gate_local * cot_ref[...].astype(F32)).astype(BF)
    qbuf[x] = q_ref[...]
    kbuf[y] = k_ref[...]
    vbuf[y] = v_ref[...]
    wfull[y, x] = w_ref[...]
    wrow[...] = jnp.zeros_like(wrow)
    pad[...] = jnp.zeros_like(pad)
    pl.semaphore_wait(barrier, len(peers))

    wa1 = [go("wa1", d - 1, w_ref.at[0:RA], wfull.at[y, x, 0:RA], X(d)) for d in (1, 2, 3)]
    wb1 = [go("wb1", d - 1, w_ref.at[RA:T], wfull.at[y, x, RA:T], Y(d)) for d in (1, 2, 3)]
    q_in = [go("q", d - 1, q_ref, qbuf.at[x], X(d)) for d in (1, 2, 3)]
    k_in = [go("k", d - 1, k_ref, kbuf.at[y], Y(d)) for d in (1, 2, 3)]
    v_in = [go("v", d - 1, v_ref, vbuf.at[y], Y(d)) for d in (1, 2, 3)]
    for peer in (twin, near):
        pl.semaphore_signal(reach.at[0], inc=1, device_id=peer, device_id_type=MESH)
    pl.semaphore_wait(reach.at[0], 2)
    for peer in (Z(1), Z(3)):
        pl.semaphore_signal(reach.at[1], inc=1, device_id=peer, device_id_type=MESH)
    pl.semaphore_wait(reach.at[1], 2)
    g_in = [go("gz", d - 1, gfull.at[ten], gfull.at[ten], Z(d)) for d in (1, 2, 3)]
    g_sib = go("gc", 0, gfull.at[ten], gfull.at[ten], sibling)

    for copy in wa1:
        copy.wait_recv()
    wa2 = [go("wa2", d - 1, wfull.at[y, :, 0:RA], wfull.at[y, :, 0:RA], Y(d)) for d in (1, 2, 3)]
    for copy in wb1:
        copy.wait_recv()
    wb2 = [go("wb2", d - 1, wfull.at[:, x, RA:T], wfull.at[:, x, RA:T], X(d)) for d in (1, 2, 3)]

    for copy in q_in:
        copy.wait_recv()
    length = len_ref[0]
    top[...] = jnp.full_like(top, MASKED)

    def score_block(j):
        rows = (j * NX + x) * T + lax.broadcasted_iota(jnp.int32, (T, 1), 0)
        live = rows < length

        def head(h, carry):
            s = dot_nt(kbuf[j, :, lanes(h)], qbuf[:, :, lanes(h)].reshape(Q, HD)) * scale
            s = jnp.where(live, s, MASKED)
            scores[h, j] = s
            top[pl.ds(h, 1), :] = jnp.maximum(
                top[pl.ds(h, 1), :], jnp.max(s, axis=0, keepdims=True)
            )
            return carry

        lax.fori_loop(0, NH, head, 0)

    score_block(y)
    for d in (3, 1, 2):
        k_in[d - 1].wait_recv()
        score_block(yi(NY - d))

    g_fwd = []
    for d in (1, 3, 2):
        g_in[d - 1].wait_recv()
        t = zi(NZ - d) * 2 + c
        g_fwd.append(go("gf", d - 1, gfull.at[t], gfull.at[t], sibling))

    for copy in v_in:
        copy.wait_recv()

    stat[x] = jnp.zeros((8, Q), F32)

    def forward_head(h, carry):
        row_top = top[pl.ds(h, 1), :]

        def block(j, total):
            p = jnp.exp(scores[h, j] - row_top)
            pbuf[j] = p.astype(BF)
            return total + jnp.sum(p, axis=0, keepdims=True)

        total = lax.fori_loop(0, NY, block, jnp.zeros((1, Q), F32))
        out_t = dot_tn(vbuf[:, :, lanes(h)].reshape(Q, HD), pbuf[...].reshape(Q, Q))
        out_t = out_t / total
        osend[:, :, lanes(h)] = out_t.T.astype(BF).reshape(NX, T, HD)
        stat[x, pl.ds(h, 1), :] = row_top + jnp.log(total)
        for d in (1, 2, 3):
            rc(
                "o", h * 3 + d - 1, osend.at[xi(d), :, lanes(h)],
                orecv.at[x, :, lanes(h)], X(d),
            ).start()
        return carry

    lax.fori_loop(0, NH, forward_head, 0)
    st_in = [go("st", d - 1, stat.at[x], stat.at[x], X(d)) for d in (1, 2, 3)]
    orecv[x] = osend[x]

    for copy in wa2 + wb2 + g_fwd + [g_sib]:
        copy.wait_recv()

    g_tile = [
        go("ga", d - 1, gfull.at[yi(d) * 2 + c], gt.at[c, y], Y(d)) for d in (1, 2, 3)
    ]
    gt[c, y] = gfull[y * 2 + c]

    def weight_rows(t):
        return wfull[lax.div(t, 2), pl.ds(lax.rem(t, 2) * 2, 2)].reshape(2 * T, DL)

    dacc[...] = jnp.zeros_like(dacc)

    def grad_step(t, carry):
        dacc[...] += dot_nn(gfull[t], weight_rows(t))
        return carry

    lax.fori_loop(0, 2 * NZ, grad_step, 0)
    dobuf[x] = dacc[...].astype(BF)
    do_in = [go("do", d - 1, dobuf.at[x], dobuf.at[x], X(d)) for d in (1, 2, 3)]

    for copy in st_in:
        copy.wait_recv()
    for h in range(NH):
        parts = [stat[j, h : h + 1, :] for j in range(NX)]
        high = functools.reduce(jnp.maximum, parts)
        row_lse = high + jnp.log(sum(jnp.exp(part - high) for part in parts))
        lse[h : h + 1, :] = row_lse
        for j in range(NX):
            wrow[h * NX + j : h * NX + j + 1, :] = jnp.exp(parts[j] - row_lse)
    wcol[...] = wrow[...].T

    def o_copy(h, d):
        return rc(
            "o", h * 3 + d - 1, osend.at[xi(d), :, lanes(h)], orecv.at[x, :, lanes(h)], X(d)
        )

    def wait_o(h, carry):
        for d in (1, 2, 3):
            o_copy(h, d).wait_recv()
        return carry

    lax.fori_loop(0, NH, wait_o, 0)
    weights = wcol[pl.ds(pl.multiple_of(x * T, 64), T), :]
    for h in range(NH):
        total = jnp.zeros((T, HD), F32)
        for j in range(NX):
            col = h * NX + j
            total += weights[:, col : col + 1] * orecv[j, :, h * HD : (h + 1) * HD].astype(F32)
        att[:, h * HD : (h + 1) * HD] = total.astype(BF)

    p_sib = {}
    for d in (2, 1, 3, 0):
        z = zi(d)
        rows = wfull[z, pl.ds((1 - c) * 2, 2)].reshape(2 * T, DL)
        psib[z] = dot_nt(att[...], rows).astype(BF)
        p_sib[d] = go("pc", d, psib.at[z], psrecv.at[z], sibling)

    attb[y] = att[...]
    at_in = [go("at", d - 1, att, attb.at[y], Y(d)) for d in (1, 2, 3)]

    pz = []
    for d in (2, 1, 3, 0):
        z = zi(d)
        rows = wfull[z, pl.ds(c * 2, 2)].reshape(2 * T, DL)
        value = dot_nt(att[...], rows)
        p_sib[d].wait_recv()
        value += psrecv[z].astype(F32)
        if d:
            pzsend[z] = value.astype(BF)
            pz.append(go("pz", d - 1, pzsend.at[z], pzrecv.at[d - 1], Z(d)))
        else:
            pown[...] = value

    lane = lax.broadcasted_iota(jnp.int32, (T, HD), 1)
    columns = jnp.zeros((T, HD), F32)
    for h in range(NH):
        sl = slice(h * HD, (h + 1) * HD)
        prod = dobuf[x, :, sl].astype(F32) * att[:, sl].astype(F32)
        columns = jnp.where(lane == h, jnp.sum(prod, axis=1, keepdims=True), columns)
    pad[pl.ds(pl.multiple_of(x * T, 64), T), :] = columns
    dls[x] = pad[...].T[0:8, :]
    dl_in = [go("dl", d - 1, dls.at[x], dls.at[x], X(d)) for d in (1, 2, 3)]

    for copy in g_tile:
        copy.wait_recv()
    g_share = go("gb", 0, gt.at[c], gt.at[c], sibling)

    for copy in do_in:
        copy.wait_recv()

    for copy in dl_in:
        copy.wait_recv()
    for h in range(NH):
        delta[h : h + 1, :] = sum(dls[j, h : h + 1, :] for j in range(NX))

    def kv_copy(name, h, d, src, dst):
        return rc(
            name, h * 3 + d - 1, src.at[yi(d), :, lanes(h)], dst.at[d - 1, :, lanes(h)], Y(d)
        )

    def q_copy(h, d):
        return rc("dq", h * 3 + d - 1, dqs.at[xi(d), :, lanes(h)], dqr.at[d - 1, :, lanes(h)], X(d))

    def backward_head(h, carry):
        row_lse = lse[pl.ds(h, 1), :]
        row_delta = delta[pl.ds(h, 1), :]
        dqacc[...] = jnp.zeros_like(dqacc)
        for d in (1, 2, 3, 0):
            j = yi(d)
            grads = dobuf[:, :, lanes(h)].reshape(Q, HD)
            p = jnp.exp(scores[h, j] - row_lse)
            dp_t = dot_nt(vbuf[j, :, lanes(h)], grads)
            ds = (p * (dp_t - row_delta) * scale).astype(BF)
            dvs[j, :, lanes(h)] = dot_nn(p.astype(BF), grads).astype(BF)
            dks[j, :, lanes(h)] = dot_nn(ds, qbuf[:, :, lanes(h)].reshape(Q, HD)).astype(BF)
            if d:
                kv_copy("dv", h, d, dvs, dvr).start()
                kv_copy("dk", h, d, dks, dkr).start()
            dqacc[...] += dot_tn(kbuf[j, :, lanes(h)], ds)
        dqs[:, :, lanes(h)] = dqacc[...].T.astype(BF).reshape(NX, T, HD)
        for d in (1, 2, 3):
            q_copy(h, d).start()
        return carry

    lax.fori_loop(0, 1, backward_head, 0)

    for copy in at_in + [g_share]:
        copy.wait_recv()
    for half in range(2):
        part = dot_tn(gt[half].reshape(NY * T, DL), attb[...].reshape(NY * T, DL))
        dw[2 * half : 2 * half + 2] = part.astype(BF).reshape(2, T, DL)
    wx = [go("wx", d - 1, dw.at[xi(d)], wxr.at[d - 1], X(d)) for d in (1, 2, 3)]

    lax.fori_loop(1, NH, backward_head, 0)

    for copy in pz:
        copy.wait_recv()
    projected = pown[...]
    for d in (1, 2, 3):
        projected += pzrecv[d - 1].astype(F32)
    br_ref[...] = (gate_local * projected).astype(BF)
    gxb[seq] = jnp.broadcast_to(
        jnp.sum(cot_ref[...].astype(F32) * projected, axis=0, keepdims=True), (8, DL)
    )
    gx = [
        go("gx", n - 1, gxb.at[seq], gxb.at[seq], {"seq": yi(n // NX) * NX + xi(n % NX)})
        for n in range(1, NX * NY)
    ]

    for copy in wx:
        copy.wait_recv()
    total = dw[x].astype(F32)
    for d in (1, 2, 3):
        total += wxr[d - 1].astype(F32)
    wdsend[...] = total.astype(BF)
    wd = go("wd", 0, wdsend, wdrecv, twin)

    def wait_grads(h, carry):
        for d in (1, 2, 3):
            kv_copy("dv", h, d, dvs, dvr).wait_recv()
            kv_copy("dk", h, d, dks, dkr).wait_recv()
            q_copy(h, d).wait_recv()
        return carry

    lax.fori_loop(0, NH, wait_grads, 0)
    for out, own, got, index in ((gv_ref, dvs, dvr, y), (gk_ref, dks, dkr, y), (gq_ref, dqs, dqr, x)):
        total = own[index].astype(F32)
        for d in (1, 2, 3):
            total += got[d - 1].astype(F32)
        out[...] = total.astype(BF)

    wd.wait_recv()
    gw_ref[...] = wdsend[...].astype(F32) + wdrecv[...].astype(F32)
    for copy in gx:
        copy.wait_recv()
    gg_ref[...] = sum(gxb[n] for n in range(NX * NY))[0:1, :]

    def wait_sends(h, carry):
        for d in (1, 2, 3):
            o_copy(h, d).wait_send()
            kv_copy("dv", h, d, dvs, dvr).wait_send()
            kv_copy("dk", h, d, dks, dkr).wait_send()
            q_copy(h, d).wait_send()
        return carry

    lax.fori_loop(0, NH, wait_sends, 0)
    for copy in sent:
        copy.wait_send()


def place(*refs):
    for i in range(6):
        refs[6 + i][...] = refs[i][...]


def shards(query_rows, key_rows, value_rows, lengths, out_weight, gate_vector, cotangent):
    T, DL = query_rows.shape[1:]
    NH = DL // HD
    Q = NX * T

    def vm(shape, dtype=BF):
        return pltpu.VMEM(shape, dtype)

    blocks = (4, T, DL)
    three = (3, T, DL)
    scratch = [
        vm(blocks), vm(blocks), vm(blocks), vm((2 * NZ, T, DL)), vm((NY, NX, T, DL)),
        vm((NH, NY, T, Q), F32), vm((NY, T, Q)), vm((8, Q), F32), vm((NX, 8, Q), F32),
        vm((8, Q), F32), vm((HD, Q), F32), vm((Q, HD), F32),
        vm(blocks), vm(blocks), vm((T, DL)), vm(blocks), vm((T, DL), F32),
        vm(blocks), vm(blocks), vm((T, DL), F32), vm(blocks), vm(three),
        vm((2, NY, T, DL)), vm(blocks), vm(blocks), vm(three),
        vm((T, DL)), vm((T, DL)), vm((NX, 8, Q), F32), vm((8, Q), F32),
        vm(blocks), vm(three), vm(blocks), vm(three), vm(blocks), vm(three), vm((HD, Q), F32),
        vm((NX * NY, 8, DL), F32),
        vm((Q, HD), F32),
        pltpu.SemaphoreType.DMA((SEM_COUNT,)), pltpu.SemaphoreType.DMA((SEM_COUNT,)),
        pltpu.SemaphoreType.REGULAR((2,)),
    ]
    vmem = pl.BlockSpec(memory_space=pltpu.VMEM)
    rows = jax.ShapeDtypeStruct((T, DL), BF)
    outs = pl.pallas_call(
        kernel,
        out_shape=(
            rows, rows, rows, rows,
            jax.ShapeDtypeStruct((T, DL), F32),
            jax.ShapeDtypeStruct((1, DL), F32),
        ),
        in_specs=[pl.BlockSpec(memory_space=pltpu.SMEM)] + [vmem] * 6,
        out_specs=(vmem,) * 6,
        scratch_shapes=scratch,
        compiler_params=pltpu.CompilerParams(
            collective_id=0, has_side_effects=True, vmem_limit_bytes=60 * 1024 * 1024
        ),
    )(lengths, query_rows[0], key_rows[0], value_rows[0], out_weight, gate_vector, cotangent[0])
    branch, grad_q, grad_k, grad_v, grad_w, grad_g = pl.pallas_call(
        place,
        out_shape=tuple(jax.ShapeDtypeStruct(out.shape, out.dtype) for out in outs),
        in_specs=[vmem] * 6,
        out_specs=(vmem,) * 6,
    )(*outs)
    return branch[None], grad_q[None], grad_k[None], grad_v[None], grad_w, grad_g


def solution(mesh):
    rows = P("dp", "seq", "tensor")
    placed = (rows, rows, rows, P("dp"), P("seq", "tensor"), P("dp", None), rows)
    return jax.shard_map(
        shards,
        mesh=mesh,
        in_specs=placed,
        out_specs=(rows, rows, rows, rows, P("seq", "tensor"), P("dp", "tensor")),
        check_vma=False,
    )
```
